32 devices in a mesh: groups: 2 (over y), beam: 16 (over z, x, core).
Axes of the slice: x: 2, y: 2, z: 4, core: 2. Of those that a mesh axis runs over, the one named last changes fastest.
Arguments:
- potential: float32 [4, 512, 512], P('groups', 'beam'), parts along dimension 0, may hold values from -5 to 5
- beam_tilts: int32 [16, 2], replicated, may hold values from -16 to 16
- aperture: float32 [16], replicated, may hold values from 0.3 to 3
- aberration: float32 [16], replicated, may hold values from -3.140625 to 3.140625
- probe_spots: int32 [8, 32, 2], P('groups'), parts along dimension 0, may hold values from 0 to 127
- crop_anchor: int32 [4], P('groups'), parts along dimension 0, may hold values from 0 to 256
Outputs:
- diffraction: float32 [1024, 32, 128], P(('groups', 'beam')), parts along dimension 0
The draws below stay inside these ranges and needn't reach their ends.
There are 2 independent parts, one for each index of `groups`. The reference program is written for one: setup_inputs(seed, part) draws one part's arguments, and reference() takes and returns one part's arrays. A program takes and returns all parts, laid end to end along the dimension named above; an argument that names none is the same for every part. Nothing has to cross between parts.
Inputs may be any that keep to these rules, and one draw needn't show every extreme that they name: `probe_spots`: positions inside a tile. `crop_anchor`: the window lies inside the grid.
All inputs are finite; a program needn't handle non-finite values.
Results may differ from the reference program's by a relative error of at most 0.0003.
Values sent between devices are 32-bit elements; how exact they have to be, the bound alone decides.
No kernel may reach another device: no remote copies, remote signals or barrier semaphores. Data moves between devices by JAX's collectives and lax.ppermute only.
A program may use at most 64 MiB of HBM per device.

```python
import math
import jax
import jax.numpy as jnp
from jax import lax

GRID = 512
CROP = 256
TILE = 128
LAYERS = 2
PROBES = 32
MAX_TILT = 16
TILES = 4
BEAMS = 16


def place_ends(array, rng, least, high):
    longest = array.shape.index(max(array.shape))
    spots = []
    for shift in (0, 1):
        where = [jax.random.randint(jax.random.fold_in(rng, axis), (), 0, length) for axis, length in enumerate(array.shape)]
        where[longest] = (where[longest] + shift) % array.shape[longest]
        spots.append(tuple(where))
    return array.at[spots[0]].set(least).at[spots[1]].set(high)


def levels(stream_key, shape, split, low, top_value):
    def one(axis_at, blocks):
        draws = jax.random.uniform(jax.random.fold_in(jax.random.fold_in(stream_key, 6), axis_at), (blocks,), jnp.float32, low / len(split), top_value / len(split))
        return jnp.repeat(jnp.exp(draws), shape[axis_at] // blocks).reshape((-1,) + (1,) * (len(shape) - axis_at - 1))

    loudness = one(*split[0])
    for cut in split[1:]:
        loudness = loudness * one(*cut)
    return loudness


def gaussian(stream_key, dims, width, reach, shards=(), held_as=jnp.bfloat16):
    drawn = jax.random.normal(stream_key, dims, jnp.float32) * width
    if len(shards) > 0:
        drawn = levels(stream_key, dims, shards, -0.22, 0.18) * drawn
    return jnp.clip(drawn, min=-reach, max=reach).astype(held_as)


def setup_inputs(seed: int = 0, part: int = 0) -> dict:
    seeds = jax.random.split(jax.random.key(seed), 7)
    part_keys = jax.random.split(jax.random.fold_in(seeds[6], part), 7)
    return {
        "potential": gaussian(part_keys[0], (LAYERS, GRID, GRID), 1.0, 5.0, ((1, 16),), jnp.float32),
        "beam_tilts": place_ends(jax.random.randint(seeds[1], (BEAMS, 2), 0 - MAX_TILT, MAX_TILT + 1), jax.random.fold_in(seeds[1], 1), 0 - MAX_TILT, MAX_TILT).astype(jnp.int32),
        "aperture": jnp.clip(jnp.exp(jax.random.uniform(seeds[2], (BEAMS,), jnp.float32, math.log(0.3), math.log(3.0))), 0.3, 3.0),
        "aberration": jnp.clip(jax.random.uniform(seeds[3], (BEAMS,), jnp.float32, -3.140625, 3.140625), -3.140625, 3.140625),
        "probe_spots": place_ends(jax.random.randint(part_keys[4], (TILES, PROBES, 2), 0, TILE), jax.random.fold_in(part_keys[4], 1), 0, TILE - 1).astype(jnp.int32),
        "crop_anchor": jax.random.randint(part_keys[5], (2,), 0, GRID - CROP + 1).astype(jnp.int32),
    }


def reference(potential, beam_tilts, aperture, aberration, probe_spots, crop_anchor):
    coords = jnp.arange(GRID, dtype=jnp.int32)
    frequency = jnp.where(coords < GRID // 2, coords, coords - GRID)
    square = frequency[:, None] ** 2 + frequency[None, :] ** 2
    phase_angle = (jnp.pi / GRID) * jnp.remainder(square, 2 * GRID).astype(jnp.float32)
    passing = 9 * square < GRID * GRID
    propagator = jnp.where(passing, jnp.cos(phase_angle) - 1j * jnp.sin(phase_angle), 0.0)
    transmit = jnp.cos(potential) + 1j * jnp.sin(potential)
    per_side = CROP // TILE

    def one_beam(tilt_pair):
        plane_phase = jnp.remainder(tilt_pair[0] * coords[:, None] + tilt_pair[1] * coords[None, :], GRID)
        plane_angle = (2.0 * jnp.pi / GRID) * plane_phase.astype(jnp.float32)
        wave_field = jnp.cos(plane_angle) + 1j * jnp.sin(plane_angle)
        for layer_index in range(LAYERS):
            wave_field = wave_field * transmit[layer_index]
            if layer_index + 1 < LAYERS:
                wave_field = jnp.fft.ifft2(propagator * jnp.fft.fft2(wave_field))
        cropped = lax.dynamic_slice(wave_field, (crop_anchor[0], crop_anchor[1]), (CROP, CROP))
        tile_stack = cropped.reshape(per_side, TILE, per_side, TILE).transpose(0, 2, 1, 3).reshape(TILES, TILE, TILE)
        return jnp.real(tile_stack), jnp.imag(tile_stack)

    beam_real, beam_imag = lax.map(one_beam, beam_tilts)
    tile_ids = jnp.arange(TILES, dtype=jnp.int32)
    anchor_rows = crop_anchor[0] + TILE * (tile_ids // per_side)
    anchor_cols = crop_anchor[1] + TILE * (tile_ids % per_side)
    spot_rows = anchor_rows[:, None] + probe_spots[:, :, 0]
    spot_cols = anchor_cols[:, None] + probe_spots[:, :, 1]
    phase_index = jnp.remainder(spot_rows[:, :, None] * beam_tilts[None, None, :, 0] + spot_cols[:, :, None] * beam_tilts[None, None, :, 1], GRID)
    weight_angle = aberration[None, None, :] - (2.0 * jnp.pi / GRID) * phase_index.astype(jnp.float32)
    weight_real = aperture[None, None, :] * jnp.cos(weight_angle)
    weight_imag = aperture[None, None, :] * jnp.sin(weight_angle)
    precise = lax.Precision.HIGHEST
    exit_real = jnp.einsum("tpb,btyx->tpyx", weight_real, beam_real, precision=precise) - jnp.einsum("tpb,btyx->tpyx", weight_imag, beam_imag, precision=precise)
    exit_imag = jnp.einsum("tpb,btyx->tpyx", weight_real, beam_imag, precision=precise) + jnp.einsum("tpb,btyx->tpyx", weight_imag, beam_real, precision=precise)
    spectrum = jnp.fft.fft2(exit_real + 1j * exit_imag)
    intensity = jnp.real(spectrum) ** 2 + jnp.imag(spectrum) ** 2
    level = jnp.mean(intensity, axis=(2, 3), keepdims=True)
    normed = intensity / (level + 1e-6)
    return normed.transpose(0, 2, 1, 3).reshape(TILES * TILE, PROBES, TILE)
```

```python
import jax
import jax.numpy as jnp
import numpy as np
from jax import lax
from jax.sharding import PartitionSpec as P

CROP = 256
TILE = 128
MAX_TILT = 16

PRECISE = lax.Precision.HIGH


def half_turn_fit():
    nodes = 0.25 * (0.5 + 0.5 * np.cos(np.pi * (np.arange(64) + 0.5) / 64))
    root = np.sqrt(nodes)
    sine = np.polynomial.chebyshev.Chebyshev.fit(nodes, np.sin(np.pi * root) / root, 5, domain=[0, 0.25])
    cosine = np.polynomial.chebyshev.Chebyshev.fit(nodes, np.cos(np.pi * root), 5, domain=[0, 0.25])
    power = np.polynomial.Polynomial
    return (
        [float(c) for c in sine.convert(kind=power).coef],
        [float(c) for c in cosine.convert(kind=power).coef],
    )


SIN_FIT, COS_FIT = half_turn_fit()


def horner(coefs, value):
    total = coefs[-1]
    for coef in coefs[-2::-1]:
        total = total * value + coef
    return total


def cis_turns(turns):
    part = turns - jnp.round(turns)
    square = part * part
    sine = part * horner(SIN_FIT, square)
    cosine = horner(COS_FIT, square)
    return 1.0 - 2.0 * sine * sine, 2.0 * sine * cosine


def cis_index(index, period):
    return cis_turns(jnp.remainder(index, period).astype(jnp.float32) * (1.0 / period))


def mul(a, b):
    return a[0] * b[0] - a[1] * b[1], a[0] * b[1] + a[1] * b[0]


def dot(left, right):
    return jnp.dot(left, right, precision=PRECISE, preferred_element_type=jnp.float32)


def times_table(field, table):
    m, n = field[0].shape[0], table[0].shape[1]
    both = dot(jnp.concatenate(field, 0), jnp.concatenate(table, 1))
    return both[:m, :n] - both[m:, n:], both[:m, n:] + both[m:, :n]


def per_device(potential, beam_tilts, aperture, aberration, probe_spots, crop_anchor, *, devices):
    layer_count, rows, length = potential.shape
    beam_count = beam_tilts.shape[0]
    per_side = CROP // TILE
    tile_count = per_side * per_side
    group = devices // tile_count
    own_beams = beam_count // group
    out_rows = tile_count * TILE // devices
    span = group * rows
    device = lax.axis_index("beam")
    my_tile = device // group
    member = device % group

    def swap(value, bits):
        return lax.ppermute(value, "beam", [(i, i ^ bits) for i in range(devices)])

    parts = length // TILE
    part_rows = rows // parts
    window = lax.dynamic_slice(potential[1], (0, crop_anchor[1]), (rows, CROP))

    def piece_for(tile):
        piece = jnp.where(tile % per_side == 0, window[:, :TILE], window[:, TILE:])
        return jnp.concatenate([piece[q * part_rows:(q + 1) * part_rows] for q in range(parts)], 1)

    def unpack(piece):
        return jnp.concatenate([piece[:, q * TILE:(q + 1) * TILE] for q in range(parts)], 0)

    blocks = [potential[0]]
    pieces = [unpack(piece_for(my_tile))]
    for shift in range(1, tile_count):
        sent = jnp.concatenate((potential[0], piece_for(my_tile ^ shift)), 0)
        got = swap(sent, shift * group)
        blocks.append(got[:rows])
        pieces.append(unpack(got[rows:]))
    anchor_row = crop_anchor[0] + TILE * (my_tile // per_side)
    anchor_col = crop_anchor[1] + TILE * (my_tile % per_side)
    inside = jnp.arange(rows, dtype=jnp.int32)
    wanted = (anchor_row + jnp.remainder(rows * member + inside - anchor_row, span)) // span
    slice_one = pieces[0]
    for shift in range(1, tile_count):
        slice_one = jnp.where((wanted == (my_tile ^ shift))[:, None], pieces[shift], slice_one)
    slice_zero = jnp.stack(blocks)[:, None]
    slice_one = slice_one[None]
    bits = group // 2
    bit_order = []
    while bits >= 1:
        count = slice_zero.shape[1]
        packed = jnp.concatenate(
            (
                slice_zero.reshape(tile_count * count * rows, length),
                jnp.concatenate(
                    [slice_one[:, q * part_rows:(q + 1) * part_rows] for q in range(parts)], 2
                ).reshape(count * part_rows, length),
            ),
            0,
        )
        got = swap(packed, bits)
        other_zero = got[: tile_count * count * rows].reshape(slice_zero.shape)
        other_one = got[tile_count * count * rows:].reshape(count, part_rows, length)
        other_one = jnp.concatenate(
            [other_one[:, :, q * TILE:(q + 1) * TILE] for q in range(parts)], 1
        )
        slice_zero = jnp.concatenate((slice_zero, other_zero), 1)
        slice_one = jnp.concatenate((slice_one, other_one), 0)
        bit_order = bit_order + [b ^ bits for b in bit_order] if bit_order else [0, bits]
        bits //= 2
    if not bit_order:
        bit_order = [0]
    offsets = jnp.asarray(np.array(bit_order, np.int32))
    member_of = member ^ offsets
    half_tiles = tile_count // 2
    slot_tile = my_tile ^ jnp.arange(half_tiles, dtype=jnp.int32)
    grid_row = (
        span * slot_tile[:, None, None] + rows * member_of[None, :, None] + inside[None, None, :]
    ).reshape(length // 2)

    half = length // 2
    kept = (length // 3 + MAX_TILT) // 64 * 64
    if kept < length // 3 + MAX_TILT:
        kept += 64
    kept = min(kept, half)
    base = jnp.arange(kept, dtype=jnp.int32) - kept // 2
    freqs = jnp.concatenate((2 * base, 2 * base + 1))
    wave = cis_turns(slice_zero.reshape(2, half, length) * (0.5 / np.pi))

    def fold(value):
        rows_even, rows_odd = value[0] + value[1], value[0] - value[1]
        stack = jnp.concatenate((rows_even, rows_odd), 0)
        return stack[:, :half] + stack[:, half:], stack[:, :half] - stack[:, half:]

    real_fold, imag_fold = fold(wave[0]), fold(wave[1])
    cols = jnp.arange(half, dtype=jnp.int32)
    spread = []
    for parity in range(2):
        table = cis_index(-cols[:, None] * (2 * base + parity)[None, :], length)
        spread.append(times_table((real_fold[parity], imag_fold[parity]), table))
    spread = [jnp.concatenate((spread[0][c], spread[1][c]), 1) for c in range(2)]
    spectrum = []
    for parity in range(2):
        table = cis_index(-(2 * base + parity)[:, None] * grid_row[None, :], length)
        rows_of = slice(parity * half, (parity + 1) * half)
        spectrum.append(times_table(table, (spread[0][rows_of], spread[1][rows_of])))
    spectrum = [jnp.concatenate((spectrum[0][c], spectrum[1][c]), 0) for c in range(2)]

    tilts = lax.dynamic_slice_in_dim(beam_tilts, member * own_beams, own_beams, 0)
    tile_rows = jnp.remainder((rows * member_of[:, None] + inside[None, :]).reshape(TILE) - anchor_row, span)
    spots_y = anchor_row + tile_rows
    offs_x = jnp.arange(TILE, dtype=jnp.int32)
    spots_x = anchor_col + offs_x
    one = cis_turns(slice_one.reshape(TILE, TILE) * (0.5 / np.pi))
    out_freq = jnp.arange(TILE, dtype=jnp.int32)
    last_x = cis_index(-offs_x[:, None] * out_freq[None, :], TILE)
    last_y = cis_index(-out_freq[:, None] * tile_rows[None, :], TILE)
    scale = 1.0 / (length * length)
    finished = []
    for b in range(own_beams):
        ky = freqs + tilts[b, 0]
        kx = freqs + tilts[b, 1]
        passing = 9 * (ky[:, None] ** 2 + kx[None, :] ** 2) < length * length
        masked = (jnp.where(passing, spectrum[0], 0.0), jnp.where(passing, spectrum[1], 0.0))
        left = cis_index(2 * ky[None, :] * spots_y[:, None] - (ky * ky)[None, :], 2 * length)
        right = cis_index(2 * kx[:, None] * spots_x[None, :] - (kx * kx)[:, None], 2 * length)
        left = (left[0] * scale, left[1] * scale)
        field = times_table(left, masked)
        field = times_table(field, right)
        field = mul(field, one)
        field = times_table(field, last_x)
        field = times_table(last_y, field)
        finished.append(jnp.stack(field))
    finished = jnp.stack(finished).reshape(own_beams * 2, TILE // out_rows, out_rows, TILE)
    finished = finished.transpose(1, 2, 0, 3)

    arrived = []
    for other in range(group):
        block = lax.dynamic_slice_in_dim(finished, member ^ other, 1, 0)[0]
        arrived.append(block if other == 0 else swap(block, other))
    arrived = jnp.concatenate(arrived, 1)
    order = (member ^ np.arange(group, dtype=np.int32))
    pick = (order[:, None] * own_beams + jnp.arange(own_beams, dtype=jnp.int32)[None, :]).reshape(beam_count)
    chosen = pick[:, None] == jnp.arange(beam_count, dtype=jnp.int32)[None, :]
    tilt_y = jnp.sum(jnp.where(chosen, beam_tilts[None, :, 0], 0), 1)
    tilt_x = jnp.sum(jnp.where(chosen, beam_tilts[None, :, 1], 0), 1)
    amplitude = jnp.sum(jnp.where(chosen, aperture[None, :], 0.0), 1)
    phase = jnp.sum(jnp.where(chosen, aberration[None, :], 0.0), 1)
    probe_here = lax.dynamic_slice_in_dim(probe_spots, my_tile, 1, 0)[0]
    spot_rows = anchor_row + probe_here[:, 0]
    spot_cols = anchor_col + probe_here[:, 1]
    index = jnp.remainder(
        spot_rows[:, None] * tilt_y[None, :] + spot_cols[:, None] * tilt_x[None, :], length
    )
    weight = cis_turns(phase[None, :] * (0.5 / np.pi) - index.astype(jnp.float32) * (1.0 / length))
    weight_real, weight_imag = amplitude[None, :] * weight[0], amplitude[None, :] * weight[1]
    probes = weight_real.shape[0]
    to_real = jnp.stack((weight_real, -weight_imag), 2).reshape(probes, 2 * beam_count)
    to_imag = jnp.stack((weight_imag, weight_real), 2).reshape(probes, 2 * beam_count)
    weights = jnp.concatenate((to_real, to_imag), 0)
    exits = jnp.einsum("pb,ybk->ypk", weights, arrived, precision=PRECISE)
    intensity = exits[:, :probes] ** 2 + exits[:, probes:] ** 2
    total = jnp.sum(intensity, (0, 2))[None, :]
    bits = 1
    while bits < group:
        total = total + swap(total, bits)
        bits *= 2
    level = total[0] / (TILE * TILE)
    return intensity / (level[None, :, None] + 1e-06)


def solution(mesh):
    placed = (P("groups", "beam", None), P(), P(), P(), P("groups", None, None), P("groups"))

    def body(*args):
        return per_device(*args, devices=mesh.shape["beam"])

    return jax.shard_map(
        body,
        mesh=mesh,
        in_specs=placed,
        out_specs=P(("groups", "beam"), None, None),
        check_vma=False,
    )
```

```python
import functools

import jax
import jax.numpy as jnp
import numpy as np
from jax import lax
from jax.experimental import pallas as pl
from jax.experimental.pallas import tpu as pltpu
from jax.sharding import PartitionSpec as P


CROP = 256
TILE = 128
MAX_TILT = 16

VMEM = pl.BlockSpec(memory_space=pltpu.VMEM)
HBM = pl.BlockSpec(memory_space=pltpu.HBM)


def half_turn_fit():
    nodes = 0.25 * (0.5 + 0.5 * np.cos(np.pi * (np.arange(64) + 0.5) / 64))
    root = np.sqrt(nodes)
    fit = np.polynomial.chebyshev.Chebyshev.fit
    sine = fit(nodes, np.sin(np.pi * root) / root, 4, domain=[0, 0.25])
    cosine = fit(nodes, np.cos(np.pi * root), 4, domain=[0, 0.25])
    power = np.polynomial.Polynomial
    return (
        [float(c) for c in sine.convert(kind=power).coef],
        [float(c) for c in cosine.convert(kind=power).coef],
    )


SIN_FIT, COS_FIT = half_turn_fit()


def horner(coefs, value):
    total = coefs[-1]
    for coef in coefs[-2::-1]:
        total = total * value + coef
    return total


def cis_part(part):
    square = part * part
    sine = part * horner(SIN_FIT, square)
    cosine = horner(COS_FIT, square)
    return 1.0 - 2.0 * sine * sine, 2.0 * sine * cosine


def cis_turns(turns):
    return cis_part(turns - jnp.floor(turns + 0.5))


def cis_index(index, period):
    part = ((index + period // 2) & (period - 1)) - period // 2
    return cis_part(part.astype(jnp.float32) * (1.0 / period))


def mul(a, b):
    return a[0] * b[0] - a[1] * b[1], a[0] * b[1] + a[1] * b[0]


def split(value):
    high = value.astype(jnp.bfloat16)
    return high, (value - high.astype(jnp.float32)).astype(jnp.bfloat16)


def dot3(left, right):
    wide = jnp.concatenate((left[0], left[1], left[0]), 1)
    tall = jnp.concatenate((right[0], right[0], right[1]), 0)
    return jnp.dot(wide, tall, preferred_element_type=jnp.float32)


def combine(both, rows, cols):
    return (
        both[:rows, :cols] - both[rows:, cols:],
        both[:rows, cols:] + both[rows:, :cols],
    )


def iota(shape, axis):
    return lax.broadcasted_iota(jnp.int32, shape, axis)


class Sizes:
    def __init__(self, devices, potential, beam_count):
        self.rows, self.length = potential[1], potential[2]
        self.beams = beam_count
        self.per_side = CROP // TILE
        self.tiles = self.per_side * self.per_side
        self.group = devices // self.tiles
        self.own = beam_count // self.group
        self.out_rows = self.tiles * TILE // devices
        self.span = self.group * self.rows
        self.half = self.length // 2
        self.pieces = self.length // TILE
        self.piece_rows = self.rows // self.pieces
        self.block = self.tiles * self.rows + self.piece_rows
        self.kept = min(-(-(self.length // 3 + MAX_TILT) // 64) * 64, self.half)
        self.freqs = 2 * self.kept
        self.chunk = min(self.group, max(1, 128 // (self.rows * self.tiles)))

    def frequency(self, position):
        kept = self.kept
        return jnp.where(position < kept, 2 * position - kept, 2 * (position - kept) - kept + 1)

    def grid_row(self, place, tile, member):
        ordinal = place // (self.rows * self.tiles // 2)
        slot = (place // self.rows) % (self.tiles // 2)
        return (
            self.span * (tile ^ slot)
            + self.rows * (member ^ ordinal)
            + place % self.rows
        )

    def tile_row(self, place, member, anchor_row):
        across = self.group * self.piece_rows
        ordinal = (place % across) // self.piece_rows
        residue = (
            self.rows * (member ^ ordinal)
            + self.piece_rows * (place // across)
            + place % self.piece_rows
        )
        return (residue - anchor_row) & (self.span - 1)

    def anchors(self, anchor_ref):
        device = lax.axis_index("beam").astype(jnp.int32)
        tile, member = device // self.group, device % self.group
        anchor_row = anchor_ref[0] + TILE * (tile // self.per_side)
        anchor_col = anchor_ref[1] + TILE * (tile % self.per_side)
        return tile, member, anchor_row, anchor_col


def put(ref, index, value, row, col):
    high, low = split(value)
    rows, cols = value.shape
    ref[index, 0, row:row + rows, col:col + cols] = high
    ref[index, 1, row:row + rows, col:col + cols] = low


def fetch(pairs, sem_ref):
    copies = [pltpu.make_async_copy(src, dst, sem_ref.at[n]) for n, (src, dst) in enumerate(pairs)]
    for copy in copies:
        copy.start()
    for copy in copies:
        copy.wait()


def pack_kernel(sizes, anchor_hbm, potential_hbm, same_ref, other_ref, anchor_ref, potential_ref, sem_ref):
    fetch(((anchor_hbm, anchor_ref), (potential_hbm, potential_ref)), sem_ref)
    tile = sizes.anchors(anchor_ref)[0]
    window = pltpu.roll(potential_ref[1], sizes.length - anchor_ref[1], 1)
    first, second = window[:, :TILE], window[:, TILE:2 * TILE]
    left = tile % sizes.per_side == 0
    rows, step = sizes.rows, sizes.piece_rows
    for ref, value in ((same_ref, jnp.where(left, first, second)), (other_ref, jnp.where(left, second, first))):
        ref[:rows] = potential_ref[0]
        for q in range(sizes.pieces):
            ref[rows:, q * TILE:(q + 1) * TILE] = value[q * step:(q + 1) * step]


def hold_kernel(sizes, anchor_hbm, *refs):
    got, (out_ref, anchor_ref, sem_ref) = refs[:-3], refs[-3:]
    fetch(((anchor_hbm, anchor_ref),), sem_ref)
    tile, member, anchor_row, _ = sizes.anchors(anchor_ref)
    rows, step = sizes.rows, sizes.piece_rows
    shape = (step, sizes.length)
    inside = step * (iota(shape, 1) // TILE) + iota(shape, 0)
    wanted = (anchor_row + ((rows * member + inside - anchor_row) & (sizes.span - 1))) // sizes.span
    piece = got[0][rows:]
    for shift, ref in enumerate(got):
        out_ref[shift * rows:(shift + 1) * rows] = ref[:rows]
        if shift:
            piece = jnp.where(wanted == (tile ^ shift), ref[rows:], piece)
    out_ref[len(got) * rows:] = piece


def column_tables(sizes):
    def both(angle, valid):
        pair = np.concatenate((np.cos(angle) * valid, np.sin(angle) * valid), 1).astype(np.float32)
        high = pair.astype(jnp.bfloat16)
        return np.stack((high, (pair - high.astype(np.float32)).astype(jnp.bfloat16)))

    half, kept = sizes.half, sizes.kept
    cols = np.arange(half)
    out = []
    for parity in range(2):
        position = cols + parity * (sizes.freqs - half)
        freq = 2 * (position - parity * kept) - kept + parity
        valid = (position < kept) if parity == 0 else (position >= kept)
        turns = (cols[:, None] * freq[None, :]) % sizes.length / sizes.length
        out.append(both(-2 * np.pi * turns, valid[None, :] * 1.0))
    cells = np.arange(TILE)
    last = both(-2 * np.pi * ((cells[:, None] * cells[None, :]) % TILE) / TILE, 1.0)
    return np.stack(out), last[None]


def tables_kernel(sizes, probes, halves, *refs):
    sources, refs = refs[:5], refs[5:]
    (rows_ref, left_ref, right_ref, mask_ref, last_y_ref, weights_ref), refs = refs[:6], refs[6:]
    fetch(tuple(zip(sources, refs[:5])), refs[5])
    anchor_ref, tilts_ref, aperture_ref, aberration_ref, spots_ref = refs[:5]
    tile, member, anchor_row, anchor_col = sizes.anchors(anchor_ref)
    half, kept, freqs, length = sizes.half, sizes.kept, sizes.freqs, sizes.length
    for parity in range(2):
        shape = (kept, half)
        freq = 2 * iota(shape, 0) - kept + parity
        place = sizes.grid_row(iota((1, half), 1), tile, member)
        pair = cis_index(-freq * place, length)
        for part in range(2):
            put(rows_ref, parity, pair[part], part * kept, 0)
    scale = 1.0 / (length * length)
    shape = (TILE, freqs)
    spot_y = anchor_row + sizes.tile_row(iota((TILE, 1), 0), member, anchor_row)
    freq_lane = sizes.frequency(iota((1, freqs), 1))
    freq_row = sizes.frequency(iota((freqs, 1), 0))
    spot_x = anchor_col + iota((1, TILE), 1)
    for b in range(sizes.own):
        beam = member * sizes.own + b
        ky = freq_lane + tilts_ref[0, beam]
        kx = freq_row + tilts_ref[1, beam]
        pair = cis_index(ky * (2 * spot_y - ky), 2 * length)
        for part in range(2):
            put(left_ref, b, pair[part] * scale, part * TILE, 0)
        pair = cis_index(kx * (2 * spot_x - kx), 2 * length)
        for part in range(2):
            put(right_ref, b, pair[part], 0, part * TILE)
        ky = freq_row + tilts_ref[0, beam]
        kx = freq_lane + tilts_ref[1, beam]
        limit = (length * length + 8) // 9
        mask_ref[b] = jnp.where(ky * ky < limit - kx * kx, 1.0, 0.0).astype(jnp.bfloat16)
    shape = (TILE, TILE)
    pair = cis_index(-iota(shape, 0) * sizes.tile_row(iota((1, TILE), 1), member, anchor_row), TILE)
    for part in range(2):
        put(last_y_ref, 0, pair[part], part * TILE, 0)
    some = sizes.own // halves
    lane = iota((1, 2 * sizes.beams), 1)
    beam = (
        (member ^ ((lane // (2 * some)) % sizes.group)) * sizes.own
        + some * (lane // (2 * some * sizes.group))
        + (lane // 2) % some
    )
    tilt_y, tilt_x = jnp.zeros_like(lane), jnp.zeros_like(lane)
    amplitude, phase = jnp.zeros(lane.shape, jnp.float32), jnp.zeros(lane.shape, jnp.float32)
    for b in range(sizes.beams):
        here = beam == b
        tilt_y = jnp.where(here, tilts_ref[0, b], tilt_y)
        tilt_x = jnp.where(here, tilts_ref[1, b], tilt_x)
        amplitude = jnp.where(here, aperture_ref[b], amplitude)
        phase = jnp.where(here, aberration_ref[b], phase)
    spots = jnp.transpose(jnp.concatenate((spots_ref[tile], jnp.zeros((6, probes), jnp.int32)), 0))
    index = (
        (anchor_row + spots[:, 0:1]) * tilt_y + (anchor_col + spots[:, 1:2]) * tilt_x
    ) & (length - 1)
    cosine, sine = cis_turns(phase * (0.5 / np.pi) - index.astype(jnp.float32) * (1.0 / length))
    even = lane % 2 == 0
    weights_ref[:probes] = amplitude * jnp.where(even, cosine, -sine)
    weights_ref[probes:] = amplitude * jnp.where(even, sine, cosine)


def spread_block(sizes, block_refs, cols_ref):
    part = sizes.tiles * sizes.rows // 2
    pairs = len(block_refs) * part
    half = sizes.half
    block = jnp.concatenate([ref[:part] for ref in block_refs] + [ref[part:2 * part] for ref in block_refs], 0)
    pieces = [ref[2 * part:] for ref in block_refs]
    wave = cis_turns(block * (0.5 / np.pi))
    folds = []
    for value in wave:
        even, odd = value[:pairs] + value[pairs:], value[:pairs] - value[pairs:]
        stack = jnp.concatenate((even, odd), 0)
        folds.append((stack[:, :half] + stack[:, half:], stack[:, :half] - stack[:, half:]))
    done = []
    for parity in range(2):
        left = split(jnp.concatenate((folds[0][parity], folds[1][parity]), 0))
        done.append(combine(dot3(left, (cols_ref[parity, 0], cols_ref[parity, 1])), 2 * pairs, half))
    shift = sizes.freqs - half
    out = []
    for c in range(2):
        low, high = done[0][c], done[1][c]
        if shift:
            out.append(jnp.concatenate((low[:, :shift], low[:, shift:] + high[:, :half - shift], high[:, half - shift:]), 1))
        else:
            out.append(low + high)
    return out, pieces


def put_pieces(sizes, ref, first, pieces):
    step = sizes.piece_rows
    for o, piece in enumerate(pieces):
        ref[(first + o) * step:(first + o + 1) * step] = piece


def spread_kernel(sizes, *refs):
    block_refs, (cols_ref, out_ref, pieces_ref) = refs[:-3], refs[-3:]
    done, pieces = spread_block(sizes, block_refs, cols_ref)
    put_pieces(sizes, pieces_ref, 0, pieces)
    pairs = out_ref.shape[2]
    for parity in range(2):
        for c in range(2):
            put(out_ref, parity, done[c][parity * pairs:(parity + 1) * pairs], 0, c * sizes.freqs)


def spectrum_kernel(sizes, earlier, *refs):
    spread_refs, pieces_refs = refs[:earlier], refs[earlier:2 * earlier]
    refs = refs[2 * earlier:]
    block_refs, (cols_ref, rows_ref, out_ref, slice_ref, pieces_ref) = refs[:-5], refs[-5:]
    done, pieces = spread_block(sizes, block_refs, cols_ref)
    start = 0
    for ref in pieces_refs:
        pieces_ref[start:start + ref.shape[0]] = ref[...]
        start += ref.shape[0]
    put_pieces(sizes, pieces_ref, start // sizes.piece_rows, pieces)
    one = cis_turns(pieces_ref[...] * (0.5 / np.pi))
    for c in range(2):
        slice_ref[c] = jnp.concatenate([one[c][:, q * TILE:(q + 1) * TILE] for q in range(sizes.pieces)], 0)
    pairs = done[0].shape[0] // 2
    freqs, kept = sizes.freqs, sizes.kept
    for parity in range(2):
        mine = split(jnp.concatenate([c[parity * pairs:(parity + 1) * pairs] for c in done], 1))
        right = [
            jnp.concatenate([ref[parity, part] for ref in spread_refs] + [mine[part]], 0) for part in range(2)
        ]
        both = dot3((rows_ref[parity, 0], rows_ref[parity, 1]), right)
        pair = combine(both, kept, freqs)
        for c in range(2):
            high, low = split(pair[c])
            out_ref[0, parity * kept:(parity + 1) * kept, c * freqs:(c + 1) * freqs] = high
            out_ref[1, parity * kept:(parity + 1) * kept, c * freqs:(c + 1) * freqs] = low


def beams_kernel(sizes, spectrum_ref, left_ref, right_ref, mask_ref, last_x_ref, last_y_ref, slice_ref, out_ref):
    freqs = sizes.freqs
    mask = jnp.concatenate((mask_ref[0], mask_ref[0]), 1)
    masked = (spectrum_ref[0] * mask, spectrum_ref[1] * mask)
    field = combine(dot3((left_ref[0, 0], left_ref[0, 1]), masked), TILE, freqs)
    field = split(jnp.concatenate(field, 0))
    field = combine(dot3(field, (right_ref[0, 0], right_ref[0, 1])), TILE, TILE)
    field = mul(field, (slice_ref[0], slice_ref[1]))
    field = split(jnp.concatenate(field, 0))
    field = combine(dot3(field, (last_x_ref[0, 0], last_x_ref[0, 1])), TILE, TILE)
    field = split(jnp.concatenate(field, 1))
    field = combine(dot3((last_y_ref[0, 0], last_y_ref[0, 1]), field), TILE, TILE)
    out_ref[0, 0] = field[0]
    out_ref[0, 1] = field[1]


def probes_kernel(sizes, probes, weights_ref, fields_ref, out_ref, sums_ref):
    inner = fields_ref.shape[0] // sizes.out_rows
    high, low = split(weights_ref[...])
    total = jnp.zeros((probes, TILE), jnp.float32)
    for row in range(sizes.out_rows):
        fields = split(fields_ref[pl.ds(row, inner, stride=sizes.out_rows), :])
        both = dot3((high, low), fields)
        intensity = both[:probes] * both[:probes] + both[probes:] * both[probes:]
        out_ref[row] = intensity
        total = total + intensity
    sums_ref[...] = jnp.broadcast_to(jnp.sum(total, 1, keepdims=True), (probes, TILE))


def scale_kernel(intensity_ref, sums_ref, out_ref):
    level = sums_ref[...] * (1.0 / (TILE * TILE)) + 1e-06
    out_ref[...] = intensity_ref[...] / level[None]


def per_device(potential, beam_tilts, aperture, aberration, probe_spots, crop_anchor, *, devices):
    sizes = Sizes(devices, potential.shape, beam_tilts.shape[0])
    rows, length, group, tiles, own = sizes.rows, sizes.length, sizes.group, sizes.tiles, sizes.own
    half, kept, freqs = sizes.half, sizes.kept, sizes.freqs
    member = lax.axis_index("beam").astype(jnp.int32) % group
    probes = probe_spots.shape[1]
    halves = 2 if own % 2 == 0 else 1
    some = own // halves

    def swap(value, bits):
        return lax.ppermute(value, "beam", [(i, i ^ bits) for i in range(devices)])

    def call(kernel, outs, specs, **kwargs):
        return pl.pallas_call(
            kernel,
            out_shape=outs,
            in_specs=specs,
            out_specs=kwargs.pop("out_specs", jax.tree.map(lambda _: VMEM, outs)),
            compiler_params=pltpu.CompilerParams(vmem_limit_bytes=16 << 20),
            **kwargs,
        )

    def half_type(*shape):
        return jax.ShapeDtypeStruct(shape, jnp.bfloat16)

    def full_type(*shape):
        return jax.ShapeDtypeStruct(shape, jnp.float32)

    def estimate(flops, bytes_accessed):
        return pl.CostEstimate(flops=flops, bytes_accessed=bytes_accessed, transcendentals=0)

    same, other_side = call(
        functools.partial(pack_kernel, sizes),
        (full_type(rows + sizes.piece_rows, length),) * 2,
        [HBM, HBM],
        scratch_shapes=[
            pltpu.SMEM(crop_anchor.shape, jnp.int32),
            pltpu.VMEM(potential.shape, jnp.float32),
            pltpu.SemaphoreType.DMA((2,)),
        ],
        cost_estimate=estimate(1 << 16, 1 << 18),
    )(crop_anchor, potential)
    blocks = [same]
    for shift in range(1, tiles):
        sent = same if shift % sizes.per_side == 0 else other_side
        blocks.append(swap(sent, shift * group))
    col_table, last_x = (jnp.asarray(table) for table in column_tables(sizes))
    row_table, left, right, masks, last_y, weights = call(
        functools.partial(tables_kernel, sizes, probes, halves),
        (
            half_type(2, 2, 2 * kept, half),
            half_type(own, 2, 2 * TILE, freqs),
            half_type(own, 2, freqs, 2 * TILE),
            half_type(own, freqs, freqs),
            half_type(1, 2, 2 * TILE, TILE),
            full_type(2 * probes, 2 * sizes.beams),
        ),
        [HBM] * 5,
        scratch_shapes=[
            pltpu.SMEM(crop_anchor.shape, jnp.int32),
            pltpu.SMEM(beam_tilts.shape[::-1], jnp.int32),
            pltpu.SMEM(aperture.shape, jnp.float32),
            pltpu.SMEM(aberration.shape, jnp.float32),
            pltpu.VMEM((tiles, 2, probes), jnp.int32),
            pltpu.SemaphoreType.DMA((5,)),
        ],
        cost_estimate=estimate(1 << 22, 6 << 20),
    )(crop_anchor, beam_tilts.T, aperture, aberration, probe_spots.transpose(0, 2, 1))
    held = call(
        functools.partial(hold_kernel, sizes),
        full_type(sizes.block, length),
        [HBM] + [VMEM] * tiles,
        scratch_shapes=[pltpu.SMEM(crop_anchor.shape, jnp.int32), pltpu.SemaphoreType.DMA((1,))],
        cost_estimate=estimate(1 << 16, 1 << 19),
    )(crop_anchor, *blocks)
    gathered = {0: held}
    for bits in member_steps(group):
        for ordinal in list(gathered):
            gathered[ordinal ^ bits] = swap(gathered[ordinal], bits)
    chunks = [
        [gathered[o] for o in range(low, low + sizes.chunk)] for low in range(0, group, sizes.chunk)
    ]

    spreads, pieces = [], []
    pairs = sizes.chunk * rows * tiles // 2
    for chunk in chunks[:-1]:
        spread, piece = call(
            functools.partial(spread_kernel, sizes),
            (half_type(2, 2, pairs, 2 * freqs), full_type(sizes.chunk * sizes.piece_rows, length)),
            [VMEM] * (sizes.chunk + 1),
            cost_estimate=estimate(pairs * half * half * 48, 2 << 20),
        )(*chunk, col_table)
        spreads.append(spread)
        pieces.append(piece)
    spectrum, slice_one = call(
        functools.partial(spectrum_kernel, sizes, len(spreads)),
        (half_type(2, freqs, 2 * freqs), full_type(2, TILE, TILE)),
        [VMEM] * (2 * len(spreads) + sizes.chunk + 2),
        cost_estimate=estimate(3 << 30, 4 << 20),
        scratch_shapes=[pltpu.VMEM((group * sizes.piece_rows, length), jnp.float32)],
    )(*spreads, *pieces, *chunks[-1], col_table, row_table)

    arrived = []
    for h in range(halves):
        table = lambda *shape: pl.BlockSpec((1,) + shape, lambda i: (h * some + i, 0, 0, 0))
        whole = lambda *shape: pl.BlockSpec(shape, lambda i: (0,) * len(shape))
        fields = call(
            functools.partial(beams_kernel, sizes),
            full_type(some, 2, TILE, TILE),
            [
                whole(2, freqs, 2 * freqs),
                table(2, 2 * TILE, freqs),
                table(2, freqs, 2 * TILE),
                pl.BlockSpec((1, freqs, freqs), lambda i: (h * some + i, 0, 0)),
                whole(1, 2, TILE, 2 * TILE),
                whole(1, 2, 2 * TILE, TILE),
                whole(2, TILE, TILE),
            ],
            grid=(some,),
            out_specs=pl.BlockSpec((1, 2, TILE, TILE), lambda i: (i, 0, 0, 0)),
            cost_estimate=pl.CostEstimate(flops=some << 30, bytes_accessed=4 << 20, transcendentals=0),
        )(spectrum, left, right, masks, last_x, last_y, slice_one)
        fields = fields.reshape(2 * some, TILE, TILE)
        for other in range(group):
            start = (member ^ other) * sizes.out_rows
            block = lax.dynamic_slice_in_dim(fields, start, sizes.out_rows, 1)
            arrived.append(block if other == 0 else swap(block, other))
    arrived = jnp.concatenate(arrived, 0).reshape(2 * sizes.beams * sizes.out_rows, TILE)

    intensity, total = call(
        functools.partial(probes_kernel, sizes, probes),
        (full_type(sizes.out_rows, probes, TILE), full_type(probes, TILE)),
        [VMEM, VMEM],
        cost_estimate=pl.CostEstimate(flops=1 << 26, bytes_accessed=2 << 20, transcendentals=0),
    )(weights, arrived)
    bits = 1
    while bits < group:
        total = total + swap(total, bits)
        bits *= 2
    return call(
        scale_kernel,
        full_type(sizes.out_rows, probes, TILE),
        [VMEM, VMEM],
        cost_estimate=pl.CostEstimate(flops=1 << 18, bytes_accessed=1 << 20, transcendentals=0),
    )(intensity, total)


def member_steps(group):
    return [group >> (i + 1) for i in range(group.bit_length() - 1)]


def solution(mesh):
    placed = (P("groups", "beam", None), P(), P(), P(), P("groups", None, None), P("groups"))

    devices = mesh.shape["beam"]

    def body(*args):
        return per_device(*args, devices=devices)

    return jax.shard_map(
        body,
        mesh=mesh,
        in_specs=placed,
        out_specs=P(("groups", "beam"), None, None),
        check_vma=False,
    )
```

```python
import functools

import jax
import jax.numpy as jnp
import numpy as np
from jax import lax
from jax.experimental import pallas as pl
from jax.experimental.pallas import tpu as pltpu
from jax.sharding import PartitionSpec as P


CROP = 256
TILE = 128
MAX_TILT = 16
STRIP = 32

VMEM = pl.BlockSpec(memory_space=pltpu.VMEM)
HBM = pl.BlockSpec(memory_space=pltpu.HBM)


def half_turn_fit():
    nodes = 0.25 * (0.5 + 0.5 * np.cos(np.pi * (np.arange(64) + 0.5) / 64))
    root = np.sqrt(nodes)
    fit = np.polynomial.chebyshev.Chebyshev.fit
    sine = fit(nodes, np.sin(np.pi * root) / root, 4, domain=[0, 0.25])
    cosine = fit(nodes, np.cos(np.pi * root), 4, domain=[0, 0.25])
    power = np.polynomial.Polynomial
    return (
        [float(c) for c in sine.convert(kind=power).coef],
        [float(c) for c in cosine.convert(kind=power).coef],
    )


SIN_FIT, COS_FIT = half_turn_fit()


def horner(coefs, value):
    total = coefs[-1]
    for coef in coefs[-2::-1]:
        total = total * value + coef
    return total


def cis_part(part):
    square = part * part
    sine = part * horner(SIN_FIT, square)
    cosine = horner(COS_FIT, square)
    return 1.0 - 2.0 * sine * sine, 2.0 * sine * cosine


def cis_turns(turns):
    return cis_part(turns - jnp.floor(turns + 0.5))


def cis_index(index, period):
    part = ((index + period // 2) & (period - 1)) - period // 2
    return cis_part(part.astype(jnp.float32) * (1.0 / period))


def mul(a, b):
    return a[0] * b[0] - a[1] * b[1], a[0] * b[1] + a[1] * b[0]


def split(value):
    high = value.astype(jnp.bfloat16)
    return high, (value - high.astype(jnp.float32)).astype(jnp.bfloat16)


def dot3(left, right):
    wide = jnp.concatenate((left[0], left[1], left[0]), 1)
    tall = jnp.concatenate((right[0], right[0], right[1]), 0)
    return jnp.dot(wide, tall, preferred_element_type=jnp.float32)


def combine(both, rows, cols):
    return (
        both[:rows, :cols] - both[rows:, cols:],
        both[:rows, cols:] + both[rows:, :cols],
    )


def iota(shape, axis):
    return lax.broadcasted_iota(jnp.int32, shape, axis)


class Sizes:
    def __init__(self, devices, potential, beam_count):
        self.rows, self.length = potential[1], potential[2]
        self.beams = beam_count
        self.per_side = CROP // TILE
        self.tiles = self.per_side * self.per_side
        self.group = devices // self.tiles
        self.own = beam_count // self.group
        self.out_rows = self.tiles * TILE // devices
        self.span = self.group * self.rows
        self.half = self.length // 2
        self.pieces = self.length // TILE
        self.piece_rows = self.rows // self.pieces
        self.block = self.tiles * self.rows + self.piece_rows
        self.kept = min(-(-(self.length // 3 + MAX_TILT) // 64) * 64, self.half)
        self.freqs = 2 * self.kept
        self.chunk = min(self.group, max(1, 128 // (self.rows * self.tiles)))

    def frequency(self, position):
        kept = self.kept
        return jnp.where(position < kept, 2 * position - kept, 2 * (position - kept) - kept + 1)

    def grid_row(self, place, tile, member):
        ordinal = place // (self.rows * self.tiles // 2)
        slot = (place // self.rows) % (self.tiles // 2)
        return (
            self.span * (tile ^ slot)
            + self.rows * (member ^ ordinal)
            + place % self.rows
        )

    def tile_row(self, place, member, anchor_row):
        across = self.group * self.piece_rows
        ordinal = (place % across) // self.piece_rows
        residue = (
            self.rows * (member ^ ordinal)
            + self.piece_rows * (place // across)
            + place % self.piece_rows
        )
        return (residue - anchor_row) & (self.span - 1)

    def anchors(self, anchor_ref):
        device = lax.axis_index("beam").astype(jnp.int32)
        tile, member = device // self.group, device % self.group
        anchor_row = anchor_ref[0] + TILE * (tile // self.per_side)
        anchor_col = anchor_ref[1] + TILE * (tile % self.per_side)
        return tile, member, anchor_row, anchor_col


def put(ref, index, value, row, col):
    high, low = split(value)
    rows, cols = value.shape
    ref[index, 0, row:row + rows, col:col + cols] = high
    ref[index, 1, row:row + rows, col:col + cols] = low


def fetch(pairs, sem_ref):
    copies = [pltpu.make_async_copy(src, dst, sem_ref.at[n]) for n, (src, dst) in enumerate(pairs)]
    for copy in copies:
        copy.start()
    for copy in copies:
        copy.wait()


def pack_kernel(sizes, anchor_hbm, potential_hbm, same_ref, other_ref, anchor_ref, potential_ref, sem_ref):
    fetch(((anchor_hbm, anchor_ref), (potential_hbm, potential_ref)), sem_ref)
    tile = sizes.anchors(anchor_ref)[0]
    window = pltpu.roll(potential_ref[1], sizes.length - anchor_ref[1], 1)
    first, second = window[:, :TILE], window[:, TILE:2 * TILE]
    left = tile % sizes.per_side == 0
    rows, step = sizes.rows, sizes.piece_rows
    for ref, value in ((same_ref, jnp.where(left, first, second)), (other_ref, jnp.where(left, second, first))):
        ref[:rows] = potential_ref[0]
        for q in range(sizes.pieces):
            ref[rows:, q * TILE:(q + 1) * TILE] = value[q * step:(q + 1) * step]


def hold_kernel(sizes, anchor_hbm, *refs):
    got, (out_ref, anchor_ref, sem_ref) = refs[:-3], refs[-3:]
    fetch(((anchor_hbm, anchor_ref),), sem_ref)
    tile, member, anchor_row, _ = sizes.anchors(anchor_ref)
    rows, step = sizes.rows, sizes.piece_rows
    shape = (step, sizes.length)
    inside = step * (iota(shape, 1) // TILE) + iota(shape, 0)
    wanted = (anchor_row + ((rows * member + inside - anchor_row) & (sizes.span - 1))) // sizes.span
    piece = got[0][rows:]
    for shift, ref in enumerate(got):
        out_ref[shift * rows:(shift + 1) * rows] = ref[:rows]
        if shift:
            piece = jnp.where(wanted == (tile ^ shift), ref[rows:], piece)
    out_ref[len(got) * rows:] = piece


def column_tables(sizes):
    def both(angle, valid):
        pair = np.concatenate((np.cos(angle) * valid, np.sin(angle) * valid), 1).astype(np.float32)
        high = pair.astype(jnp.bfloat16)
        return np.stack((high, (pair - high.astype(np.float32)).astype(jnp.bfloat16)))

    half, kept = sizes.half, sizes.kept
    cols = np.arange(half)
    out = []
    for parity in range(2):
        position = cols + parity * (sizes.freqs - half)
        freq = 2 * (position - parity * kept) - kept + parity
        valid = (position < kept) if parity == 0 else (position >= kept)
        turns = (cols[:, None] * freq[None, :]) % sizes.length / sizes.length
        out.append(both(-2 * np.pi * turns, valid[None, :] * 1.0))
    cells = np.arange(TILE)
    last = both(-2 * np.pi * ((cells[:, None] * cells[None, :]) % TILE) / TILE, 1.0)
    return np.stack(out), last[None]


def tables_kernel(sizes, probes, halves, *refs):
    sources, refs = refs[:5], refs[5:]
    (rows_ref, left_ref, right_ref, mask_ref, last_y_ref, weights_ref), refs = refs[:6], refs[6:]
    fetch(tuple(zip(sources, refs[:5])), refs[5])
    anchor_ref, tilts_ref, aperture_ref, aberration_ref, spots_ref = refs[:5]
    tile, member, anchor_row, anchor_col = sizes.anchors(anchor_ref)
    half, kept, freqs, length = sizes.half, sizes.kept, sizes.freqs, sizes.length
    place = sizes.grid_row(iota((1, half), 1), tile, member)
    step = cis_index(-place, length)
    for top in range(0, kept, STRIP):
        freq = 2 * (iota((STRIP, 1), 0) + top) - kept
        pair = cis_index(-freq * place, length)
        for parity in range(2):
            for part in range(2):
                put(rows_ref, parity, pair[part], part * kept + top, 0)
            pair = mul(pair, step)
    scale = 1.0 / (length * length)
    freq_lane = sizes.frequency(iota((1, freqs), 1))
    spot_x = anchor_col + iota((1, TILE), 1)
    limit = (length * length + 8) // 9
    beams = [member * sizes.own + b for b in range(sizes.own)]
    tilt_y = [tilts_ref[0, beam] for beam in beams]
    tilt_x = [tilts_ref[1, beam] for beam in beams]
    chirps = []
    for t in tilt_y:
        ky = freq_lane + t
        chirps.append(cis_index(-ky * ky, 2 * length))
    for top in range(0, TILE, STRIP):
        spot_y = anchor_row + sizes.tile_row(iota((STRIP, 1), 0) + top, member, anchor_row)
        common = [value * scale for value in cis_index(freq_lane * spot_y, length)]
        for b in range(sizes.own):
            pair = mul(mul(common, chirps[b]), cis_index(tilt_y[b] * spot_y, length))
            for part in range(2):
                put(left_ref, b, pair[part], part * TILE + top, 0)
    starts = [cis_index(t * spot_x, length) for t in tilt_x]
    squares = []
    for t in tilt_x:
        kx = freq_lane + t
        squares.append(limit - kx * kx)
    for top in range(0, freqs, STRIP):
        freq_row = sizes.frequency(iota((STRIP, 1), 0) + top)
        common = cis_index(freq_row * spot_x, length)
        for b in range(sizes.own):
            kx = freq_row + tilt_x[b]
            pair = mul(mul(common, cis_index(-kx * kx, 2 * length)), starts[b])
            for part in range(2):
                put(right_ref, b, pair[part], top, part * TILE)
            ky = freq_row + tilt_y[b]
            mask_ref[b, top:top + STRIP] = jnp.where(ky * ky < squares[b], 1.0, 0.0).astype(jnp.bfloat16)
    shape = (TILE, TILE)
    pair = cis_index(-iota(shape, 0) * sizes.tile_row(iota((1, TILE), 1), member, anchor_row), TILE)
    for part in range(2):
        put(last_y_ref, 0, pair[part], part * TILE, 0)
    some = sizes.own // halves
    lane = iota((1, 2 * sizes.beams), 1)
    beam = (
        (member ^ ((lane // (2 * some)) % sizes.group)) * sizes.own
        + some * (lane // (2 * some * sizes.group))
        + (lane // 2) % some
    )
    tilt_y, tilt_x = jnp.zeros_like(lane), jnp.zeros_like(lane)
    amplitude, phase = jnp.zeros(lane.shape, jnp.float32), jnp.zeros(lane.shape, jnp.float32)
    for b in range(sizes.beams):
        here = beam == b
        tilt_y = jnp.where(here, tilts_ref[0, b], tilt_y)
        tilt_x = jnp.where(here, tilts_ref[1, b], tilt_x)
        amplitude = jnp.where(here, aperture_ref[b], amplitude)
        phase = jnp.where(here, aberration_ref[b], phase)
    spots = jnp.transpose(jnp.concatenate((spots_ref[tile], jnp.zeros((6, probes), jnp.int32)), 0))
    index = (
        (anchor_row + spots[:, 0:1]) * tilt_y + (anchor_col + spots[:, 1:2]) * tilt_x
    ) & (length - 1)
    cosine, sine = cis_turns(phase * (0.5 / np.pi) - index.astype(jnp.float32) * (1.0 / length))
    even = lane % 2 == 0
    weights_ref[:probes] = amplitude * jnp.where(even, cosine, -sine)
    weights_ref[probes:] = amplitude * jnp.where(even, sine, cosine)


def spread_block(sizes, block_refs, cols_ref):
    part = sizes.tiles * sizes.rows // 2
    pairs = len(block_refs) * part
    half = sizes.half
    block = jnp.concatenate([ref[:part] for ref in block_refs] + [ref[part:2 * part] for ref in block_refs], 0)
    pieces = [ref[2 * part:] for ref in block_refs]
    wave = cis_turns(block * (0.5 / np.pi))
    folds = []
    for value in wave:
        even, odd = value[:pairs] + value[pairs:], value[:pairs] - value[pairs:]
        stack = jnp.concatenate((even, odd), 0)
        folds.append((stack[:, :half] + stack[:, half:], stack[:, :half] - stack[:, half:]))
    done = []
    for parity in range(2):
        left = split(jnp.concatenate((folds[0][parity], folds[1][parity]), 0))
        done.append(combine(dot3(left, (cols_ref[parity, 0], cols_ref[parity, 1])), 2 * pairs, half))
    shift = sizes.freqs - half
    out = []
    for c in range(2):
        low, high = done[0][c], done[1][c]
        if shift:
            out.append(jnp.concatenate((low[:, :shift], low[:, shift:] + high[:, :half - shift], high[:, half - shift:]), 1))
        else:
            out.append(low + high)
    return out, pieces


def put_pieces(sizes, ref, first, pieces):
    step = sizes.piece_rows
    for o, piece in enumerate(pieces):
        ref[(first + o) * step:(first + o + 1) * step] = piece


def spread_kernel(sizes, *refs):
    block_refs, (cols_ref, out_ref, pieces_ref) = refs[:-3], refs[-3:]
    done, pieces = spread_block(sizes, block_refs, cols_ref)
    put_pieces(sizes, pieces_ref, 0, pieces)
    pairs = out_ref.shape[2]
    for parity in range(2):
        for c in range(2):
            put(out_ref, parity, done[c][parity * pairs:(parity + 1) * pairs], 0, c * sizes.freqs)


def spectrum_kernel(sizes, earlier, *refs):
    spread_refs, pieces_refs = refs[:earlier], refs[earlier:2 * earlier]
    refs = refs[2 * earlier:]
    block_refs, (cols_ref, rows_ref, out_ref, slice_ref, pieces_ref) = refs[:-5], refs[-5:]
    done, pieces = spread_block(sizes, block_refs, cols_ref)
    start = 0
    for ref in pieces_refs:
        pieces_ref[start:start + ref.shape[0]] = ref[...]
        start += ref.shape[0]
    put_pieces(sizes, pieces_ref, start // sizes.piece_rows, pieces)
    one = cis_turns(pieces_ref[...] * (0.5 / np.pi))
    for c in range(2):
        slice_ref[c] = jnp.concatenate([one[c][:, q * TILE:(q + 1) * TILE] for q in range(sizes.pieces)], 0)
    pairs = done[0].shape[0] // 2
    freqs, kept = sizes.freqs, sizes.kept
    for parity in range(2):
        mine = split(jnp.concatenate([c[parity * pairs:(parity + 1) * pairs] for c in done], 1))
        right = [
            jnp.concatenate([ref[parity, part] for ref in spread_refs] + [mine[part]], 0) for part in range(2)
        ]
        both = dot3((rows_ref[parity, 0], rows_ref[parity, 1]), right)
        pair = combine(both, kept, freqs)
        for c in range(2):
            high, low = split(pair[c])
            out_ref[0, parity * kept:(parity + 1) * kept, c * freqs:(c + 1) * freqs] = high
            out_ref[1, parity * kept:(parity + 1) * kept, c * freqs:(c + 1) * freqs] = low


def beams_kernel(sizes, first, spectrum_ref, left_ref, right_ref, mask_ref, last_x_ref, last_y_ref, slice_ref, *refs):
    out_refs, field_ref = refs[:-1], refs[-1]
    freqs = sizes.freqs
    some = field_ref.shape[0] // 2
    member = lax.axis_index("beam").astype(jnp.int32) % sizes.group
    for b in range(some):
        mask = mask_ref[first + b]
        mask = jnp.concatenate((mask, mask), 1)
        masked = (spectrum_ref[0] * mask, spectrum_ref[1] * mask)
        field = combine(dot3((left_ref[first + b, 0], left_ref[first + b, 1]), masked), TILE, freqs)
        field = split(jnp.concatenate(field, 0))
        field = combine(dot3(field, (right_ref[first + b, 0], right_ref[first + b, 1])), TILE, TILE)
        field = mul(field, (slice_ref[0], slice_ref[1]))
        field = split(jnp.concatenate(field, 0))
        field = combine(dot3(field, (last_x_ref[0, 0], last_x_ref[0, 1])), TILE, TILE)
        field = split(jnp.concatenate(field, 1))
        field = combine(dot3((last_y_ref[0, 0], last_y_ref[0, 1]), field), TILE, TILE)
        for c in range(2):
            field_ref[2 * b + c] = field[c]
    for other, out_ref in enumerate(out_refs):
        start = pl.multiple_of((member ^ other) * sizes.out_rows, sizes.out_rows)
        for n in range(2 * some):
            out_ref[n * sizes.out_rows:(n + 1) * sizes.out_rows] = field_ref[n, pl.ds(start, sizes.out_rows), :]


def probes_kernel(sizes, probes, weights_ref, *refs):
    field_refs, (out_ref, sums_ref, fields_ref) = refs[:-3], refs[-3:]
    count = field_refs[0].shape[0]
    for n, ref in enumerate(field_refs):
        fields_ref[n * count:(n + 1) * count] = ref[...]
    inner = fields_ref.shape[0] // sizes.out_rows
    weights = split(weights_ref[...])
    total = jnp.zeros((probes, TILE), jnp.float32)
    for row in range(sizes.out_rows):
        fields = split(fields_ref[pl.ds(row, inner, stride=sizes.out_rows), :])
        both = dot3(weights, fields)
        intensity = both[:probes] * both[:probes] + both[probes:] * both[probes:]
        out_ref[row] = intensity
        total = total + intensity
    sums_ref[...] = jnp.broadcast_to(jnp.sum(total, 1, keepdims=True), (probes, TILE))


def scale_kernel(intensity_ref, *refs):
    sums_refs, out_ref = refs[:-1], refs[-1]
    level = sums_refs[0][...]
    for ref in sums_refs[1:]:
        level = level + ref[...]
    level = level * (1.0 / (TILE * TILE)) + 1e-06
    out_ref[...] = intensity_ref[...] / level[None]


def per_device(potential, beam_tilts, aperture, aberration, probe_spots, crop_anchor, *, devices):
    sizes = Sizes(devices, potential.shape, beam_tilts.shape[0])
    rows, length, group, tiles, own = sizes.rows, sizes.length, sizes.group, sizes.tiles, sizes.own
    half, kept, freqs = sizes.half, sizes.kept, sizes.freqs
    member = lax.axis_index("beam").astype(jnp.int32) % group
    probes = probe_spots.shape[1]
    halves = 2 if own % 2 == 0 else 1
    some = own // halves

    def swap(value, bits):
        return lax.ppermute(value, "beam", [(i, i ^ bits) for i in range(devices)])

    def call(kernel, outs, specs, **kwargs):
        return pl.pallas_call(
            kernel,
            out_shape=outs,
            in_specs=specs,
            out_specs=kwargs.pop("out_specs", jax.tree.map(lambda _: VMEM, outs)),
            compiler_params=pltpu.CompilerParams(vmem_limit_bytes=16 << 20),
            **kwargs,
        )

    def half_type(*shape):
        return jax.ShapeDtypeStruct(shape, jnp.bfloat16)

    def full_type(*shape):
        return jax.ShapeDtypeStruct(shape, jnp.float32)

    def estimate(flops, bytes_accessed):
        return pl.CostEstimate(flops=flops, bytes_accessed=bytes_accessed, transcendentals=0)

    same, other_side = call(
        functools.partial(pack_kernel, sizes),
        (full_type(rows + sizes.piece_rows, length),) * 2,
        [HBM, HBM],
        scratch_shapes=[
            pltpu.SMEM(crop_anchor.shape, jnp.int32),
            pltpu.VMEM(potential.shape, jnp.float32),
            pltpu.SemaphoreType.DMA((2,)),
        ],
        cost_estimate=estimate(1 << 16, 1 << 18),
    )(crop_anchor, potential)
    blocks = [same]
    for shift in range(1, tiles):
        sent = same if shift % sizes.per_side == 0 else other_side
        blocks.append(swap(sent, shift * group))
    col_table, last_x = (jnp.asarray(table) for table in column_tables(sizes))
    row_table, left, right, masks, last_y, weights = call(
        functools.partial(tables_kernel, sizes, probes, halves),
        (
            half_type(2, 2, 2 * kept, half),
            half_type(own, 2, 2 * TILE, freqs),
            half_type(own, 2, freqs, 2 * TILE),
            half_type(own, freqs, freqs),
            half_type(1, 2, 2 * TILE, TILE),
            full_type(2 * probes, 2 * sizes.beams),
        ),
        [HBM] * 5,
        scratch_shapes=[
            pltpu.SMEM(crop_anchor.shape, jnp.int32),
            pltpu.SMEM(beam_tilts.shape[::-1], jnp.int32),
            pltpu.SMEM(aperture.shape, jnp.float32),
            pltpu.SMEM(aberration.shape, jnp.float32),
            pltpu.VMEM((tiles, 2, probes), jnp.int32),
            pltpu.SemaphoreType.DMA((5,)),
        ],
        cost_estimate=estimate(1 << 22, 6 << 20),
    )(crop_anchor, beam_tilts.T, aperture, aberration, probe_spots.transpose(0, 2, 1))
    held = call(
        functools.partial(hold_kernel, sizes),
        full_type(sizes.block, length),
        [HBM] + [VMEM] * tiles,
        scratch_shapes=[pltpu.SMEM(crop_anchor.shape, jnp.int32), pltpu.SemaphoreType.DMA((1,))],
        cost_estimate=estimate(1 << 16, 1 << 19),
    )(crop_anchor, *blocks)
    gathered = {0: held}
    for bits in member_steps(group):
        for ordinal in list(gathered):
            gathered[ordinal ^ bits] = swap(gathered[ordinal], bits)
    chunks = [
        [gathered[o] for o in range(low, low + sizes.chunk)] for low in range(0, group, sizes.chunk)
    ]

    spreads, pieces = [], []
    pairs = sizes.chunk * rows * tiles // 2
    for chunk in chunks[:-1]:
        spread, piece = call(
            functools.partial(spread_kernel, sizes),
            (half_type(2, 2, pairs, 2 * freqs), full_type(sizes.chunk * sizes.piece_rows, length)),
            [VMEM] * (sizes.chunk + 1),
            cost_estimate=estimate(pairs * half * half * 48, 2 << 20),
        )(*chunk, col_table)
        spreads.append(spread)
        pieces.append(piece)
    spectrum, slice_one = call(
        functools.partial(spectrum_kernel, sizes, len(spreads)),
        (half_type(2, freqs, 2 * freqs), full_type(2, TILE, TILE)),
        [VMEM] * (2 * len(spreads) + sizes.chunk + 2),
        cost_estimate=estimate(3 << 30, 4 << 20),
        scratch_shapes=[pltpu.VMEM((group * sizes.piece_rows, length), jnp.float32)],
    )(*spreads, *pieces, *chunks[-1], col_table, row_table)

    arrived = []
    for h in range(halves):
        fields = call(
            functools.partial(beams_kernel, sizes, h * some),
            (full_type(2 * some * sizes.out_rows, TILE),) * group,
            [VMEM] * 7,
            scratch_shapes=[pltpu.VMEM((2 * some, TILE, TILE), jnp.float32)],
            cost_estimate=estimate(some << 30, 4 << 20),
        )(spectrum, left, right, masks, last_x, last_y, slice_one)
        arrived.append(fields[0])
        for other in range(1, group):
            arrived.append(swap(fields[other], other))

    intensity, total = call(
        functools.partial(probes_kernel, sizes, probes),
        (full_type(sizes.out_rows, probes, TILE), full_type(probes, TILE)),
        [VMEM] * (1 + len(arrived)),
        scratch_shapes=[pltpu.VMEM((2 * sizes.beams * sizes.out_rows, TILE), jnp.float32)],
        cost_estimate=estimate(1 << 26, 2 << 20),
    )(weights, *arrived)
    totals = [total]
    if group <= 4:
        for other in range(1, group):
            totals.append(swap(total, other))
    else:
        for bits in member_steps(group):
            total = total + swap(total, bits)
        totals = [total]
    return call(
        scale_kernel,
        full_type(sizes.out_rows, probes, TILE),
        [VMEM] * (1 + len(totals)),
        cost_estimate=estimate(1 << 18, 1 << 20),
    )(intensity, *totals)


def member_steps(group):
    return [group >> (i + 1) for i in range(group.bit_length() - 1)]


def solution(mesh):
    placed = (P("groups", "beam", None), P(), P(), P(), P("groups", None, None), P("groups"))

    devices = mesh.shape["beam"]

    def body(*args):
        return per_device(*args, devices=devices)

    return jax.shard_map(
        body,
        mesh=mesh,
        in_specs=placed,
        out_specs=P(("groups", "beam"), None, None),
        check_vma=False,
    )
```

```python
import functools

import jax
import jax.numpy as jnp
import numpy as np
from jax import lax
from jax.experimental import pallas as pl
from jax.experimental.pallas import tpu as pltpu
from jax.sharding import PartitionSpec as P


CROP = 256
TILE = 128
MAX_TILT = 16
STRIP = 32

VMEM = pl.BlockSpec(memory_space=pltpu.VMEM)
HBM = pl.BlockSpec(memory_space=pltpu.HBM)


def half_turn_fit():
    nodes = 0.25 * (0.5 + 0.5 * np.cos(np.pi * (np.arange(64) + 0.5) / 64))
    root = np.sqrt(nodes)
    fit = np.polynomial.chebyshev.Chebyshev.fit
    sine = fit(nodes, np.sin(np.pi * root) / root, 4, domain=[0, 0.25])
    cosine = fit(nodes, np.cos(np.pi * root), 4, domain=[0, 0.25])
    power = np.polynomial.Polynomial
    return (
        [float(c) for c in sine.convert(kind=power).coef],
        [float(c) for c in cosine.convert(kind=power).coef],
    )


SIN_FIT, COS_FIT = half_turn_fit()


def horner(coefs, value):
    total = coefs[-1]
    for coef in coefs[-2::-1]:
        total = total * value + coef
    return total


def cis_part(part):
    square = part * part
    sine = part * horner(SIN_FIT, square)
    cosine = horner(COS_FIT, square)
    return 1.0 - 2.0 * sine * sine, 2.0 * sine * cosine


def cis_turns(turns):
    return cis_part(turns - jnp.floor(turns + 0.5))


def cis_index(index, period):
    return cis_turns(index.astype(jnp.float32) * (1.0 / period))


def mul(a, b):
    return a[0] * b[0] - a[1] * b[1], a[0] * b[1] + a[1] * b[0]


def split(value):
    high = value.astype(jnp.bfloat16)
    return high, (value - high.astype(jnp.float32)).astype(jnp.bfloat16)


def dot3(left, right):
    wide = jnp.concatenate((left[0], left[1], left[0]), 1)
    tall = jnp.concatenate((right[0], right[0], right[1]), 0)
    return jnp.dot(wide, tall, preferred_element_type=jnp.float32)


def combine(both, rows, cols):
    return (
        both[:rows, :cols] - both[rows:, cols:],
        both[:rows, cols:] + both[rows:, :cols],
    )


def iota(shape, axis):
    return lax.broadcasted_iota(jnp.int32, shape, axis)


class Sizes:
    def __init__(self, devices, potential, beam_count):
        self.rows, self.length = potential[1], potential[2]
        self.beams = beam_count
        self.per_side = CROP // TILE
        self.tiles = self.per_side * self.per_side
        self.group = devices // self.tiles
        self.share = 1
        while self.share < self.group and beam_count // self.share > 8:
            self.share *= 2
        self.own = beam_count // self.share
        self.out_rows = self.tiles * TILE // devices
        self.span = self.group * self.rows
        self.half = self.length // 2
        self.pieces = self.length // TILE
        self.piece_rows = self.rows // self.pieces
        self.block = self.tiles * self.rows + self.piece_rows
        self.kept = min(-(-(self.length // 3 + MAX_TILT) // 64) * 64, self.half)
        self.freqs = 2 * self.kept
        self.chunk = min(self.group, max(1, 128 // (self.rows * self.tiles)))

    def frequency(self, position):
        kept = self.kept
        return jnp.where(position < kept, 2 * position - kept, 2 * (position - kept) - kept + 1)

    def grid_row(self, place, tile, member):
        ordinal = place // (self.rows * self.tiles // 2)
        slot = (place // self.rows) % (self.tiles // 2)
        return (
            self.span * (tile ^ slot)
            + self.rows * (member ^ ordinal)
            + place % self.rows
        )

    def tile_row(self, place, member, anchor_row):
        across = self.group * self.piece_rows
        ordinal = (place % across) // self.piece_rows
        residue = (
            self.rows * (member ^ ordinal)
            + self.piece_rows * (place // across)
            + place % self.piece_rows
        )
        return (residue - anchor_row) & (self.span - 1)

    def anchors(self, anchor_ref):
        device = lax.axis_index("beam").astype(jnp.int32)
        tile, member = device // self.group, device % self.group
        anchor_row = anchor_ref[0] + TILE * (tile // self.per_side)
        anchor_col = anchor_ref[1] + TILE * (tile % self.per_side)
        return tile, member, anchor_row, anchor_col


def put(ref, index, value, row, col):
    high, low = split(value)
    rows, cols = value.shape
    ref[index, 0, row:row + rows, col:col + cols] = high
    ref[index, 1, row:row + rows, col:col + cols] = low


def fetch(pairs, sem_ref):
    copies = [pltpu.make_async_copy(src, dst, sem_ref.at[n]) for n, (src, dst) in enumerate(pairs)]
    for copy in copies:
        copy.start()
    for copy in copies:
        copy.wait()


def pack_kernel(sizes, anchor_hbm, potential_hbm, same_ref, other_ref, anchor_ref, potential_ref, sem_ref):
    fetch(((anchor_hbm, anchor_ref), (potential_hbm, potential_ref)), sem_ref)
    tile = sizes.anchors(anchor_ref)[0]
    window = pltpu.roll(potential_ref[1], sizes.length - anchor_ref[1], 1)
    first, second = window[:, :TILE], window[:, TILE:2 * TILE]
    left = tile % sizes.per_side == 0
    rows, step = sizes.rows, sizes.piece_rows
    for ref, value in ((same_ref, jnp.where(left, first, second)), (other_ref, jnp.where(left, second, first))):
        ref[:rows] = potential_ref[0]
        for q in range(sizes.pieces):
            ref[rows:, q * TILE:(q + 1) * TILE] = value[q * step:(q + 1) * step]


def hold_kernel(sizes, anchor_hbm, *refs):
    got, (out_ref, anchor_ref, sem_ref) = refs[:-3], refs[-3:]
    fetch(((anchor_hbm, anchor_ref),), sem_ref)
    tile, member, anchor_row, _ = sizes.anchors(anchor_ref)
    rows, step = sizes.rows, sizes.piece_rows
    shape = (step, sizes.length)
    inside = step * (iota(shape, 1) // TILE) + iota(shape, 0)
    wanted = (anchor_row + ((rows * member + inside - anchor_row) & (sizes.span - 1))) // sizes.span
    piece = got[0][rows:]
    for shift, ref in enumerate(got):
        out_ref[shift * rows:(shift + 1) * rows] = ref[:rows]
        if shift:
            piece = jnp.where(wanted == (tile ^ shift), ref[rows:], piece)
    out_ref[len(got) * rows:] = piece


def column_tables(sizes):
    def both(angle, valid):
        pair = np.concatenate((np.cos(angle) * valid, np.sin(angle) * valid), 1).astype(np.float32)
        high = pair.astype(jnp.bfloat16)
        return np.stack((high, (pair - high.astype(np.float32)).astype(jnp.bfloat16)))

    half, kept = sizes.half, sizes.kept
    cols = np.arange(half)
    out = []
    for parity in range(2):
        position = cols + parity * (sizes.freqs - half)
        freq = 2 * (position - parity * kept) - kept + parity
        valid = (position < kept) if parity == 0 else (position >= kept)
        turns = (cols[:, None] * freq[None, :]) % sizes.length / sizes.length
        out.append(both(-2 * np.pi * turns, valid[None, :] * 1.0))
    cells = np.arange(TILE)
    last = both(-2 * np.pi * ((cells[:, None] * cells[None, :]) % TILE) / TILE, 1.0)
    return np.stack(out), last[None]


def whole(value):
    return value.astype(jnp.float32)


def early_tables_kernel(sizes, probes, halves, anchor_hbm, small_hbm, *refs):
    (rows_ref, left_ref, last_y_ref, incident_ref, weights_ref), (anchor_ref, small_ref, spots_ref, sem_ref) = refs[:5], refs[5:]
    fetch(((anchor_hbm, anchor_ref), (small_hbm, small_ref), (small_hbm, spots_ref)), sem_ref)
    tile, member, anchor_row, anchor_col = sizes.anchors(anchor_ref)
    half, kept, freqs, length = sizes.half, sizes.kept, sizes.freqs, sizes.length
    place = whole(sizes.grid_row(iota((1, half), 1), tile, member))
    step = cis_index(-place, length)
    for top in range(0, kept, STRIP):
        freq = whole(2 * (iota((STRIP, 1), 0) + top) - kept)
        pair = cis_index(-freq * place, length)
        for parity in range(2):
            for part in range(2):
                put(rows_ref, parity, pair[part], part * kept + top, 0)
            if parity == 0:
                pair = mul(pair, step)
    scale = 1.0 / (length * length)
    freq_lane = whole(sizes.frequency(iota((1, freqs), 1)))
    beams = [(member % sizes.share) * sizes.own + b for b in range(sizes.own)]
    tilt_y = [small_ref[0, beam] for beam in beams]
    tilt_x = [small_ref[1, beam] for beam in beams]
    chirps = []
    for t in tilt_y:
        ky = freq_lane + t
        chirps.append([value * scale for value in cis_index(-ky * ky, 2 * length)])
    lane = iota((1, TILE), 1)
    packed = jnp.zeros((1, TILE), jnp.float32)
    for b, t in enumerate(tilt_y):
        packed = jnp.where(lane == b, t, packed)
    spot_x = whole(anchor_col + lane)
    starts = [cis_index(t * spot_x, length) for t in tilt_x]
    for top in range(0, TILE, STRIP):
        spot_y = whole(anchor_row + sizes.tile_row(iota((STRIP, 1), 0) + top, member, anchor_row))
        common = cis_index(freq_lane * spot_y, length)
        turn = cis_index(packed * spot_y, length)
        for b in range(sizes.own):
            pair = mul(common, chirps[b])
            side = mul((turn[0][:, b:b + 1], turn[1][:, b:b + 1]), starts[b])
            for part in range(2):
                put(left_ref, b, pair[part], part * TILE + top, 0)
                incident_ref[b, part, top:top + STRIP] = side[part]
    shape = (TILE, TILE)
    pair = cis_index(
        -whole(iota(shape, 0)) * whole(sizes.tile_row(iota((1, TILE), 1), member, anchor_row)), TILE
    )
    for part in range(2):
        put(last_y_ref, 0, pair[part], part * TILE, 0)
    some = sizes.own // halves
    lane = iota((1, 2 * sizes.beams), 1)
    beam = (
        ((member % sizes.share) ^ ((lane // (2 * some)) % sizes.share)) * sizes.own
        + some * (lane // (2 * some * sizes.share))
        + (lane // 2) % some
    )
    zero = jnp.zeros(lane.shape, jnp.float32)
    picked = [zero] * 4
    for b in range(sizes.beams):
        here = beam == b
        picked = [jnp.where(here, small_ref[n, b], value) for n, value in enumerate(picked)]
    spots = spots_ref[pl.ds(4 + 2 * tile, 2), :probes]
    spots = jnp.transpose(jnp.concatenate((spots, jnp.zeros((6, probes), jnp.float32)), 0))
    index = (whole(anchor_row) + spots[:, 0:1]) * picked[0] + (whole(anchor_col) + spots[:, 1:2]) * picked[1]
    index = index * (1.0 / length)
    index = index - jnp.floor(index)
    cosine, sine = cis_turns(picked[3] * (0.5 / np.pi) - index)
    even = lane % 2 == 0
    weights_ref[:probes] = picked[2] * jnp.where(even, cosine, -sine)
    weights_ref[probes:] = picked[2] * jnp.where(even, sine, cosine)


def late_tables_kernel(sizes, anchor_hbm, small_hbm, right_ref, mask_ref, anchor_ref, small_ref, sem_ref):
    fetch(((anchor_hbm, anchor_ref), (small_hbm, small_ref)), sem_ref)
    _, member, _, anchor_col = sizes.anchors(anchor_ref)
    freqs, length = sizes.freqs, sizes.length
    beams = [(member % sizes.share) * sizes.own + b for b in range(sizes.own)]
    lane = iota((1, TILE), 1)
    spot_x = whole(anchor_col + lane)
    packed_x, packed_y = jnp.zeros((1, TILE), jnp.float32), jnp.zeros((1, TILE), jnp.float32)
    freq_lane = whole(sizes.frequency(iota((1, freqs), 1)))
    limit = float((length * length + 8) // 9)
    squares = []
    for b, beam in enumerate(beams):
        packed_y = jnp.where(lane == b, small_ref[0, beam], packed_y)
        packed_x = jnp.where(lane == b, small_ref[1, beam], packed_x)
        kx = freq_lane + small_ref[1, beam]
        squares.append(limit - kx * kx)
    for top in range(0, freqs, STRIP):
        freq_row = whole(sizes.frequency(iota((STRIP, 1), 0) + top))
        common = cis_index(freq_row * spot_x, length)
        kx = freq_row + packed_x
        chirp = cis_index(-kx * kx, 2 * length)
        ky = freq_row + packed_y
        square = ky * ky
        for b in range(sizes.own):
            pair = mul(common, (chirp[0][:, b:b + 1], chirp[1][:, b:b + 1]))
            for part in range(2):
                put(right_ref, b, pair[part], top, part * TILE)
            mask_ref[b, top:top + STRIP] = jnp.where(square[:, b:b + 1] < squares[b], 1.0, 0.0).astype(jnp.bfloat16)


def spread_block(sizes, block_refs, cols_ref):
    part = sizes.tiles * sizes.rows // 2
    pairs = len(block_refs) * part
    half = sizes.half
    block = jnp.concatenate([ref[:part] for ref in block_refs] + [ref[part:2 * part] for ref in block_refs], 0)
    pieces = [ref[2 * part:] for ref in block_refs]
    wave = cis_turns(block * (0.5 / np.pi))
    folds = []
    for value in wave:
        even, odd = value[:pairs] + value[pairs:], value[:pairs] - value[pairs:]
        stack = jnp.concatenate((even, odd), 0)
        folds.append((stack[:, :half] + stack[:, half:], stack[:, :half] - stack[:, half:]))
    done = []
    for parity in range(2):
        left = split(jnp.concatenate((folds[0][parity], folds[1][parity]), 0))
        done.append(combine(dot3(left, (cols_ref[parity, 0], cols_ref[parity, 1])), 2 * pairs, half))
    shift = sizes.freqs - half
    out = []
    for c in range(2):
        low, high = done[0][c], done[1][c]
        if shift:
            out.append(jnp.concatenate((low[:, :shift], low[:, shift:] + high[:, :half - shift], high[:, half - shift:]), 1))
        else:
            out.append(low + high)
    return out, pieces


def put_pieces(sizes, ref, first, pieces):
    step = sizes.piece_rows
    for o, piece in enumerate(pieces):
        ref[(first + o) * step:(first + o + 1) * step] = piece


def spread_kernel(sizes, *refs):
    block_refs, (cols_ref, out_ref, pieces_ref) = refs[:-3], refs[-3:]
    done, pieces = spread_block(sizes, block_refs, cols_ref)
    put_pieces(sizes, pieces_ref, 0, pieces)
    pairs = out_ref.shape[2]
    for parity in range(2):
        for c in range(2):
            put(out_ref, parity, done[c][parity * pairs:(parity + 1) * pairs], 0, c * sizes.freqs)


def spectrum_kernel(sizes, earlier, *refs):
    spread_refs, pieces_refs = refs[:earlier], refs[earlier:2 * earlier]
    refs = refs[2 * earlier:]
    block_refs, (cols_ref, rows_ref, out_ref, slice_ref, pieces_ref) = refs[:-5], refs[-5:]
    done, pieces = spread_block(sizes, block_refs, cols_ref)
    start = 0
    for ref in pieces_refs:
        pieces_ref[start:start + ref.shape[0]] = ref[...]
        start += ref.shape[0]
    put_pieces(sizes, pieces_ref, start // sizes.piece_rows, pieces)
    one = cis_turns(pieces_ref[...] * (0.5 / np.pi))
    for c in range(2):
        slice_ref[c] = jnp.concatenate([one[c][:, q * TILE:(q + 1) * TILE] for q in range(sizes.pieces)], 0)
    pairs = done[0].shape[0] // 2
    freqs, kept = sizes.freqs, sizes.kept
    for parity in range(2):
        mine = split(jnp.concatenate([c[parity * pairs:(parity + 1) * pairs] for c in done], 1))
        right = [
            jnp.concatenate([ref[parity, part] for ref in spread_refs] + [mine[part]], 0) for part in range(2)
        ]
        both = dot3((rows_ref[parity, 0], rows_ref[parity, 1]), right)
        pair = combine(both, kept, freqs)
        for c in range(2):
            high, low = split(pair[c])
            out_ref[0, parity * kept:(parity + 1) * kept, c * freqs:(c + 1) * freqs] = high
            out_ref[1, parity * kept:(parity + 1) * kept, c * freqs:(c + 1) * freqs] = low


def beams_kernel(sizes, first, spectrum_ref, left_ref, right_ref, mask_ref, last_x_ref, last_y_ref, slice_ref, incident_ref, *refs):
    out_refs, field_ref = refs[:-1], refs[-1]
    freqs = sizes.freqs
    some = field_ref.shape[0] // 2
    member = lax.axis_index("beam").astype(jnp.int32) % sizes.group
    names = range(first, first + some)
    fields = []
    for b in names:
        mask = jnp.concatenate((mask_ref[b], mask_ref[b]), 1)
        masked = (spectrum_ref[0] * mask, spectrum_ref[1] * mask)
        field = combine(dot3((left_ref[b, 0], left_ref[b, 1]), masked), TILE, freqs)
        fields.append(split(jnp.concatenate(field, 0)))
    ends = []
    for b, field in zip(names, fields):
        field = combine(dot3(field, (right_ref[b, 0], right_ref[b, 1])), TILE, TILE)
        field = mul(field, mul((slice_ref[0], slice_ref[1]), (incident_ref[b, 0], incident_ref[b, 1])))
        ends.append(split(jnp.concatenate(field, 0)))
    turned = []
    for field in ends:
        field = combine(dot3(field, (last_x_ref[0, 0], last_x_ref[0, 1])), TILE, TILE)
        turned.append(split(jnp.concatenate(field, 1)))
    for n, field in enumerate(turned):
        field = combine(dot3((last_y_ref[0, 0], last_y_ref[0, 1]), field), TILE, TILE)
        for c in range(2):
            field_ref[2 * n + c] = field[c]
    rows = sizes.out_rows
    sets = sizes.group // sizes.share
    for other, out_ref in enumerate(out_refs):
        for k in range(sets):
            start = pl.multiple_of((member ^ other ^ (sizes.share * k)) * rows, rows)
            for n in range(2 * some):
                out_ref[k, n * rows:(n + 1) * rows] = field_ref[n, pl.ds(start, rows), :]


def probes_kernel(sizes, probes, weights_ref, *refs):
    field_refs, (out_ref, sums_ref, fields_ref) = refs[:-3], refs[-3:]
    sets, count = field_refs[0].shape[:2]
    for n, ref in enumerate(field_refs):
        for k in range(sets):
            fields_ref[k, n * count:(n + 1) * count] = ref[k]
    inner = fields_ref.shape[1] // sizes.out_rows
    weights = split(weights_ref[...])
    total = jnp.zeros((probes, TILE), jnp.float32)
    for k in range(sets):
        for row in range(sizes.out_rows):
            fields = split(fields_ref[k, pl.ds(row, inner, stride=sizes.out_rows), :])
            both = dot3(weights, fields)
            intensity = both[:probes] * both[:probes] + both[probes:] * both[probes:]
            if k == 0:
                out_ref[row] = intensity
            total = total + intensity
    sums_ref[...] = jnp.broadcast_to(jnp.sum(total, 1, keepdims=True), (probes, TILE))


def scale_kernel(intensity_ref, *refs):
    sums_refs, out_ref = refs[:-1], refs[-1]
    level = sums_refs[0][...]
    for ref in sums_refs[1:]:
        level = level + ref[...]
    level = level * (1.0 / (TILE * TILE)) + 1e-06
    out_ref[...] = intensity_ref[...] / level[None]


def per_device(potential, beam_tilts, aperture, aberration, probe_spots, crop_anchor, *, devices):
    sizes = Sizes(devices, potential.shape, beam_tilts.shape[0])
    rows, length, group, tiles, own = sizes.rows, sizes.length, sizes.group, sizes.tiles, sizes.own
    half, kept, freqs = sizes.half, sizes.kept, sizes.freqs
    member = lax.axis_index("beam").astype(jnp.int32) % group
    probes = probe_spots.shape[1]
    halves = 2 if own % 2 == 0 else 1
    some = own // halves

    def swap(value, bits):
        return lax.ppermute(value, "beam", [(i, i ^ bits) for i in range(devices)])

    def call(kernel, outs, specs, **kwargs):
        return pl.pallas_call(
            kernel,
            out_shape=outs,
            in_specs=specs,
            out_specs=kwargs.pop("out_specs", jax.tree.map(lambda _: VMEM, outs)),
            compiler_params=pltpu.CompilerParams(vmem_limit_bytes=16 << 20),
            **kwargs,
        )

    def half_type(*shape):
        return jax.ShapeDtypeStruct(shape, jnp.bfloat16)

    def full_type(*shape):
        return jax.ShapeDtypeStruct(shape, jnp.float32)

    def estimate(flops, bytes_accessed):
        return pl.CostEstimate(flops=flops, bytes_accessed=bytes_accessed, transcendentals=0)

    same, other_side = call(
        functools.partial(pack_kernel, sizes),
        (full_type(rows + sizes.piece_rows, length),) * 2,
        [HBM, HBM],
        scratch_shapes=[
            pltpu.SMEM(crop_anchor.shape, jnp.int32),
            pltpu.VMEM(potential.shape, jnp.float32),
            pltpu.SemaphoreType.DMA((2,)),
        ],
        cost_estimate=estimate(1 << 16, 1 << 18),
    )(crop_anchor, potential)
    blocks = [same]
    for shift in range(1, tiles):
        sent = same if shift % sizes.per_side == 0 else other_side
        blocks.append(swap(sent, shift * group))
    col_table, last_x = (jnp.asarray(table) for table in column_tables(sizes))
    small = pack_small(sizes, beam_tilts, aperture, aberration, probe_spots)
    fetched = [pltpu.SMEM(crop_anchor.shape, jnp.int32), pltpu.SMEM(small.shape, jnp.float32)]
    row_table, left, last_y, incident, weights = call(
        functools.partial(early_tables_kernel, sizes, probes, halves),
        (
            half_type(2, 2, 2 * kept, half),
            half_type(own, 2, 2 * TILE, freqs),
            half_type(1, 2, 2 * TILE, TILE),
            full_type(own, 2, TILE, TILE),
            full_type(2 * probes, 2 * sizes.beams),
        ),
        [HBM] * 2,
        scratch_shapes=fetched + [pltpu.VMEM(small.shape, jnp.float32), pltpu.SemaphoreType.DMA((3,))],
        cost_estimate=estimate(1 << 22, 6 << 20),
    )(crop_anchor, small)
    right, masks = call(
        functools.partial(late_tables_kernel, sizes),
        (half_type(own, 2, freqs, 2 * TILE), half_type(own, freqs, freqs)),
        [HBM] * 2,
        scratch_shapes=fetched + [pltpu.SemaphoreType.DMA((2,))],
        cost_estimate=estimate(1 << 22, 6 << 20),
    )(crop_anchor, small)
    held = call(
        functools.partial(hold_kernel, sizes),
        full_type(sizes.block, length),
        [HBM] + [VMEM] * tiles,
        scratch_shapes=[pltpu.SMEM(crop_anchor.shape, jnp.int32), pltpu.SemaphoreType.DMA((1,))],
        cost_estimate=estimate(1 << 16, 1 << 19),
    )(crop_anchor, *blocks)
    gathered = {0: held}
    for bits in member_steps(group):
        for ordinal in list(gathered):
            gathered[ordinal ^ bits] = swap(gathered[ordinal], bits)
    chunks = [
        [gathered[o] for o in range(low, low + sizes.chunk)] for low in range(0, group, sizes.chunk)
    ]

    spreads, pieces = [], []
    pairs = sizes.chunk * rows * tiles // 2
    for chunk in chunks[:-1]:
        spread, piece = call(
            functools.partial(spread_kernel, sizes),
            (half_type(2, 2, pairs, 2 * freqs), full_type(sizes.chunk * sizes.piece_rows, length)),
            [VMEM] * (sizes.chunk + 1),
            cost_estimate=estimate(pairs * half * half * 48, 2 << 20),
        )(*chunk, col_table)
        spreads.append(spread)
        pieces.append(piece)
    spectrum, slice_one = call(
        functools.partial(spectrum_kernel, sizes, len(spreads)),
        (half_type(2, freqs, 2 * freqs), full_type(2, TILE, TILE)),
        [VMEM] * (2 * len(spreads) + sizes.chunk + 2),
        cost_estimate=estimate(3 << 30, 4 << 20),
        scratch_shapes=[pltpu.VMEM((group * sizes.piece_rows, length), jnp.float32)],
    )(*spreads, *pieces, *chunks[-1], col_table, row_table)

    arrived = []
    sets = group // sizes.share
    for h in range(halves):
        fields = call(
            functools.partial(beams_kernel, sizes, h * some),
            (full_type(sets, 2 * some * sizes.out_rows, TILE),) * sizes.share,
            [VMEM] * 8,
            scratch_shapes=[pltpu.VMEM((2 * some, TILE, TILE), jnp.float32)],
            cost_estimate=estimate(some << 30, 4 << 20),
        )(spectrum, left, right, masks, last_x, last_y, slice_one, incident)
        arrived.append(fields[0])
        for other in range(1, sizes.share):
            arrived.append(swap(fields[other], other))

    intensity, total = call(
        functools.partial(probes_kernel, sizes, probes),
        (full_type(sizes.out_rows, probes, TILE), full_type(probes, TILE)),
        [VMEM] * (1 + len(arrived)),
        scratch_shapes=[pltpu.VMEM((sets, 2 * sizes.beams * sizes.out_rows, TILE), jnp.float32)],
        cost_estimate=estimate(1 << 26, 2 << 20),
    )(weights, *arrived)
    totals = [total]
    if sizes.share <= 4:
        for other in range(1, sizes.share):
            totals.append(swap(total, other))
    else:
        for bits in member_steps(sizes.share):
            total = total + swap(total, bits)
        totals = [total]
    return call(
        scale_kernel,
        full_type(sizes.out_rows, probes, TILE),
        [VMEM] * (1 + len(totals)),
        cost_estimate=estimate(1 << 18, 1 << 20),
    )(intensity, *totals)


def pack_small(sizes, beam_tilts, aperture, aberration, probe_spots):
    probes = probe_spots.shape[1]
    width = max(sizes.beams, probes)
    spots = probe_spots.transpose(0, 2, 1).reshape(2 * sizes.tiles, probes).astype(jnp.float32)
    beams = jnp.concatenate((beam_tilts.T.astype(jnp.float32), aperture[None], aberration[None]), 0)
    return jnp.concatenate(
        (
            jnp.pad(beams, ((0, 0), (0, width - sizes.beams))),
            jnp.pad(spots, ((0, 0), (0, width - probes))),
        ),
        0,
    )


def member_steps(group):
    return [group >> (i + 1) for i in range(group.bit_length() - 1)]


def solution(mesh):
    placed = (P("groups", "beam", None), P(), P(), P(), P("groups", None, None), P("groups"))

    devices = mesh.shape["beam"]

    def body(*args):
        return per_device(*args, devices=devices)

    return jax.shard_map(
        body,
        mesh=mesh,
        in_specs=placed,
        out_specs=P(("groups", "beam"), None, None),
        check_vma=False,
    )
```

```python
import functools

import jax
import jax.numpy as jnp
import numpy as np
from jax import lax
from jax.experimental import pallas as pl
from jax.experimental.pallas import tpu as pltpu
from jax.sharding import PartitionSpec as P


CROP = 256
TILE = 128
MAX_TILT = 16
STRIP = 32

VMEM = pl.BlockSpec(memory_space=pltpu.VMEM)
HBM = pl.BlockSpec(memory_space=pltpu.HBM)


def half_turn_fit():
    nodes = 0.25 * (0.5 + 0.5 * np.cos(np.pi * (np.arange(64) + 0.5) / 64))
    root = np.sqrt(nodes)
    fit = np.polynomial.chebyshev.Chebyshev.fit
    sine = fit(nodes, np.sin(np.pi * root) / root, 4, domain=[0, 0.25])
    cosine = fit(nodes, np.cos(np.pi * root), 4, domain=[0, 0.25])
    power = np.polynomial.Polynomial
    return (
        [float(c) for c in sine.convert(kind=power).coef],
        [float(c) for c in cosine.convert(kind=power).coef],
    )


SIN_FIT, COS_FIT = half_turn_fit()


def horner(coefs, value):
    total = coefs[-1]
    for coef in coefs[-2::-1]:
        total = total * value + coef
    return total


def cis_part(part):
    square = part * part
    sine = part * horner(SIN_FIT, square)
    cosine = horner(COS_FIT, square)
    return 1.0 - 2.0 * sine * sine, 2.0 * sine * cosine


def cis_turns(turns):
    return cis_part(turns - jnp.floor(turns + 0.5))


def cis_index(index, period):
    return cis_turns(index.astype(jnp.float32) * (1.0 / period))


def mul(a, b):
    return a[0] * b[0] - a[1] * b[1], a[0] * b[1] + a[1] * b[0]


def split(value):
    high = value.astype(jnp.bfloat16)
    return high, (value - high.astype(jnp.float32)).astype(jnp.bfloat16)


def dot3(left, right):
    wide = jnp.concatenate((left[0], left[1], left[0]), 1)
    tall = jnp.concatenate((right[0], right[0], right[1]), 0)
    return jnp.dot(wide, tall, preferred_element_type=jnp.float32)


def combine(both, rows, cols):
    return (
        both[:rows, :cols] - both[rows:, cols:],
        both[:rows, cols:] + both[rows:, :cols],
    )


def iota(shape, axis):
    return lax.broadcasted_iota(jnp.int32, shape, axis)


class Sizes:
    def __init__(self, devices, potential, beam_count):
        self.rows, self.length = potential[1], potential[2]
        self.beams = beam_count
        self.per_side = CROP // TILE
        self.tiles = self.per_side * self.per_side
        self.group = devices // self.tiles
        self.share = 1
        while self.share < self.group and beam_count // self.share > 8:
            self.share *= 2
        self.own = beam_count // self.share
        self.out_rows = self.tiles * TILE // devices
        self.span = self.group * self.rows
        self.half = self.length // 2
        self.pieces = self.length // TILE
        self.piece_rows = self.rows // self.pieces
        self.block = self.tiles * self.rows + self.piece_rows
        self.kept = min(-(-(self.length // 3 + MAX_TILT) // 64) * 64, self.half)
        self.freqs = 2 * self.kept
        self.chunk = min(self.group, max(1, 128 // (self.rows * self.tiles)))

    def frequency(self, position):
        kept = self.kept
        return jnp.where(position < kept, 2 * position - kept, 2 * (position - kept) - kept + 1)

    def grid_row(self, place, tile, member):
        ordinal = place // (self.rows * self.tiles // 2)
        slot = (place // self.rows) % (self.tiles // 2)
        return (
            self.span * (tile ^ slot)
            + self.rows * (member ^ ordinal)
            + place % self.rows
        )

    def tile_row(self, place, member, anchor_row):
        across = self.group * self.piece_rows
        ordinal = (place % across) // self.piece_rows
        residue = (
            self.rows * (member ^ ordinal)
            + self.piece_rows * (place // across)
            + place % self.piece_rows
        )
        return (residue - anchor_row) & (self.span - 1)

    def anchors(self, anchor_ref):
        device = lax.axis_index("beam").astype(jnp.int32)
        tile, member = device // self.group, device % self.group
        anchor_row = anchor_ref[0] + TILE * (tile // self.per_side)
        anchor_col = anchor_ref[1] + TILE * (tile % self.per_side)
        return tile, member, anchor_row, anchor_col


def put(ref, index, value, row, col):
    high, low = split(value)
    rows, cols = value.shape
    ref[index, 0, row:row + rows, col:col + cols] = high
    ref[index, 1, row:row + rows, col:col + cols] = low


def fetch(pairs, sem_ref):
    copies = [pltpu.make_async_copy(src, dst, sem_ref.at[n]) for n, (src, dst) in enumerate(pairs)]
    for copy in copies:
        copy.start()
    for copy in copies:
        copy.wait()


def pack_kernel(sizes, anchor_ref, potential_ref, same_ref, other_ref):
    tile = lax.axis_index("beam").astype(jnp.int32) // sizes.group
    anchors = anchor_ref[...]
    column = jnp.sum(jnp.where(iota(anchors.shape, 1) == 1, anchors, 0).astype(jnp.float32)).astype(jnp.int32)
    window = pltpu.roll(potential_ref[1], sizes.length - column, 1)
    first, second = window[:, :TILE], window[:, TILE:2 * TILE]
    left = tile % sizes.per_side == 0
    rows, step = sizes.rows, sizes.piece_rows
    for ref, value in ((same_ref, jnp.where(left, first, second)), (other_ref, jnp.where(left, second, first))):
        ref[:rows] = potential_ref[0]
        for q in range(sizes.pieces):
            ref[rows:, q * TILE:(q + 1) * TILE] = value[q * step:(q + 1) * step]


def hold_kernel(sizes, choice_ref, *refs):
    got, out_ref = refs[:-1], refs[-1]
    rows = sizes.rows
    choice = choice_ref[...]
    piece = got[0][rows:]
    for shift, ref in enumerate(got):
        out_ref[shift * rows:(shift + 1) * rows] = ref[:rows]
        if shift:
            piece = jnp.where(choice == shift, ref[rows:], piece)
    out_ref[len(got) * rows:] = piece


def column_tables(sizes):
    def both(angle, valid):
        pair = np.concatenate((np.cos(angle) * valid, np.sin(angle) * valid), 1).astype(np.float32)
        high = pair.astype(jnp.bfloat16)
        return np.stack((high, (pair - high.astype(np.float32)).astype(jnp.bfloat16)))

    half, kept = sizes.half, sizes.kept
    cols = np.arange(half)
    out = []
    for parity in range(2):
        position = cols + parity * (sizes.freqs - half)
        freq = 2 * (position - parity * kept) - kept + parity
        valid = (position < kept) if parity == 0 else (position >= kept)
        turns = (cols[:, None] * freq[None, :]) % sizes.length / sizes.length
        out.append(both(-2 * np.pi * turns, valid[None, :] * 1.0))
    cells = np.arange(TILE)
    last = both(-2 * np.pi * ((cells[:, None] * cells[None, :]) % TILE) / TILE, 1.0)
    return np.stack(out), last[None]


def whole(value):
    return value.astype(jnp.float32)


def early_tables_kernel(sizes, probes, halves, anchor_hbm, small_hbm, *refs):
    choice_ref, rows_ref, left_ref, last_y_ref, incident_ref, weights_ref = refs[:6]
    anchor_ref, small_ref, spots_ref, sem_ref = refs[6:]
    fetch(((anchor_hbm, anchor_ref), (small_hbm, small_ref), (small_hbm, spots_ref)), sem_ref)
    tile, member, anchor_row, anchor_col = sizes.anchors(anchor_ref)
    half, kept, freqs, length = sizes.half, sizes.kept, sizes.freqs, sizes.length
    shape = (sizes.piece_rows, length)
    inside = sizes.piece_rows * (iota(shape, 1) // TILE) + iota(shape, 0)
    residue = (sizes.rows * member + inside - anchor_row) & (sizes.span - 1)
    choice_ref[...] = ((anchor_row + residue) // sizes.span) ^ tile
    place = whole(sizes.grid_row(iota((1, half), 1), tile, member))
    step = cis_index(-place, length)
    for top in range(0, kept, STRIP):
        freq = whole(2 * (iota((STRIP, 1), 0) + top) - kept)
        pair = cis_index(-freq * place, length)
        for parity in range(2):
            for part in range(2):
                put(rows_ref, parity, pair[part], part * kept + top, 0)
            if parity == 0:
                pair = mul(pair, step)
    scale = 1.0 / (length * length)
    freq_lane = whole(sizes.frequency(iota((1, freqs), 1)))
    beams = [(member % sizes.share) * sizes.own + b for b in range(sizes.own)]
    tilt_y = [small_ref[0, beam] for beam in beams]
    tilt_x = [small_ref[1, beam] for beam in beams]
    chirps = []
    for t in tilt_y:
        ky = freq_lane + t
        chirps.append([value * scale for value in cis_index(-ky * ky, 2 * length)])
    lane = iota((1, TILE), 1)
    packed = jnp.zeros((1, TILE), jnp.float32)
    for b, t in enumerate(tilt_y):
        packed = jnp.where(lane == b, t, packed)
    spot_x = whole(anchor_col + lane)
    starts = [cis_index(t * spot_x, length) for t in tilt_x]
    for top in range(0, TILE, STRIP):
        spot_y = whole(anchor_row + sizes.tile_row(iota((STRIP, 1), 0) + top, member, anchor_row))
        common = cis_index(freq_lane * spot_y, length)
        turn = cis_index(packed * spot_y, length)
        for b in range(sizes.own):
            pair = mul(common, chirps[b])
            side = mul((turn[0][:, b:b + 1], turn[1][:, b:b + 1]), starts[b])
            for part in range(2):
                put(left_ref, b, pair[part], part * TILE + top, 0)
                incident_ref[b, part, top:top + STRIP] = side[part]
    shape = (TILE, TILE)
    pair = cis_index(
        -whole(iota(shape, 0)) * whole(sizes.tile_row(iota((1, TILE), 1), member, anchor_row)), TILE
    )
    for part in range(2):
        put(last_y_ref, 0, pair[part], part * TILE, 0)
    some = sizes.own // halves
    lane = iota((1, 2 * sizes.beams), 1)
    beam = (
        ((member % sizes.share) ^ ((lane // (2 * some)) % sizes.share)) * sizes.own
        + some * (lane // (2 * some * sizes.share))
        + (lane // 2) % some
    )
    zero = jnp.zeros(lane.shape, jnp.float32)
    picked = [zero] * 4
    for b in range(sizes.beams):
        here = beam == b
        picked = [jnp.where(here, small_ref[n, b], value) for n, value in enumerate(picked)]
    spots = spots_ref[pl.ds(4 + 2 * tile, 2), :probes]
    spots = jnp.transpose(jnp.concatenate((spots, jnp.zeros((6, probes), jnp.float32)), 0))
    index = (whole(anchor_row) + spots[:, 0:1]) * picked[0] + (whole(anchor_col) + spots[:, 1:2]) * picked[1]
    index = index * (1.0 / length)
    index = index - jnp.floor(index)
    cosine, sine = cis_turns(picked[3] * (0.5 / np.pi) - index)
    even = lane % 2 == 0
    weights_ref[:probes] = picked[2] * jnp.where(even, cosine, -sine)
    weights_ref[probes:] = picked[2] * jnp.where(even, sine, cosine)


def late_tables_kernel(sizes, anchor_hbm, small_hbm, right_ref, mask_ref, anchor_ref, small_ref, sem_ref):
    fetch(((anchor_hbm, anchor_ref), (small_hbm, small_ref)), sem_ref)
    _, member, _, anchor_col = sizes.anchors(anchor_ref)
    freqs, length = sizes.freqs, sizes.length
    beams = [(member % sizes.share) * sizes.own + b for b in range(sizes.own)]
    lane = iota((1, TILE), 1)
    spot_x = whole(anchor_col + lane)
    packed_x, packed_y = jnp.zeros((1, TILE), jnp.float32), jnp.zeros((1, TILE), jnp.float32)
    freq_lane = whole(sizes.frequency(iota((1, freqs), 1)))
    limit = float((length * length + 8) // 9)
    squares = []
    for b, beam in enumerate(beams):
        packed_y = jnp.where(lane == b, small_ref[0, beam], packed_y)
        packed_x = jnp.where(lane == b, small_ref[1, beam], packed_x)
        kx = freq_lane + small_ref[1, beam]
        squares.append(limit - kx * kx)
    for top in range(0, freqs, STRIP):
        freq_row = whole(sizes.frequency(iota((STRIP, 1), 0) + top))
        common = cis_index(freq_row * spot_x, length)
        kx = freq_row + packed_x
        chirp = cis_index(-kx * kx, 2 * length)
        ky = freq_row + packed_y
        square = ky * ky
        for b in range(sizes.own):
            pair = mul(common, (chirp[0][:, b:b + 1], chirp[1][:, b:b + 1]))
            for part in range(2):
                put(right_ref, b, pair[part], top, part * TILE)
            mask_ref[b, top:top + STRIP] = jnp.where(square[:, b:b + 1] < squares[b], 1.0, 0.0).astype(jnp.bfloat16)


def spread_block(sizes, block_refs, cols_ref):
    part = sizes.tiles * sizes.rows // 2
    pairs = len(block_refs) * part
    half = sizes.half
    block = jnp.concatenate([ref[:part] for ref in block_refs] + [ref[part:2 * part] for ref in block_refs], 0)
    pieces = [ref[2 * part:] for ref in block_refs]
    wave = cis_turns(block * (0.5 / np.pi))
    folds = []
    for value in wave:
        even, odd = value[:pairs] + value[pairs:], value[:pairs] - value[pairs:]
        stack = jnp.concatenate((even, odd), 0)
        folds.append((stack[:, :half] + stack[:, half:], stack[:, :half] - stack[:, half:]))
    done = []
    for parity in range(2):
        left = split(jnp.concatenate((folds[0][parity], folds[1][parity]), 0))
        done.append(combine(dot3(left, (cols_ref[parity, 0], cols_ref[parity, 1])), 2 * pairs, half))
    shift = sizes.freqs - half
    out = []
    for c in range(2):
        low, high = done[0][c], done[1][c]
        if shift:
            out.append(jnp.concatenate((low[:, :shift], low[:, shift:] + high[:, :half - shift], high[:, half - shift:]), 1))
        else:
            out.append(low + high)
    return out, pieces


def put_pieces(sizes, ref, first, pieces):
    step = sizes.piece_rows
    for o, piece in enumerate(pieces):
        ref[(first + o) * step:(first + o + 1) * step] = piece


def spread_kernel(sizes, *refs):
    block_refs, (cols_ref, out_ref, pieces_ref) = refs[:-3], refs[-3:]
    done, pieces = spread_block(sizes, block_refs, cols_ref)
    put_pieces(sizes, pieces_ref, 0, pieces)
    pairs = out_ref.shape[2]
    for parity in range(2):
        for c in range(2):
            put(out_ref, parity, done[c][parity * pairs:(parity + 1) * pairs], 0, c * sizes.freqs)


def spectrum_kernel(sizes, earlier, *refs):
    spread_refs, pieces_refs = refs[:earlier], refs[earlier:2 * earlier]
    refs = refs[2 * earlier:]
    block_refs, (cols_ref, rows_ref, out_ref, slice_ref, pieces_ref) = refs[:-5], refs[-5:]
    done, pieces = spread_block(sizes, block_refs, cols_ref)
    start = 0
    for ref in pieces_refs:
        pieces_ref[start:start + ref.shape[0]] = ref[...]
        start += ref.shape[0]
    put_pieces(sizes, pieces_ref, start // sizes.piece_rows, pieces)
    one = cis_turns(pieces_ref[...] * (0.5 / np.pi))
    for c in range(2):
        slice_ref[c] = jnp.concatenate([one[c][:, q * TILE:(q + 1) * TILE] for q in range(sizes.pieces)], 0)
    pairs = done[0].shape[0] // 2
    freqs, kept = sizes.freqs, sizes.kept
    for parity in range(2):
        mine = split(jnp.concatenate([c[parity * pairs:(parity + 1) * pairs] for c in done], 1))
        right = [
            jnp.concatenate([ref[parity, part] for ref in spread_refs] + [mine[part]], 0) for part in range(2)
        ]
        both = dot3((rows_ref[parity, 0], rows_ref[parity, 1]), right)
        pair = combine(both, kept, freqs)
        for c in range(2):
            high, low = split(pair[c])
            out_ref[0, parity * kept:(parity + 1) * kept, c * freqs:(c + 1) * freqs] = high
            out_ref[1, parity * kept:(parity + 1) * kept, c * freqs:(c + 1) * freqs] = low


def beams_kernel(sizes, first, spectrum_ref, left_ref, right_ref, mask_ref, last_x_ref, last_y_ref, slice_ref, incident_ref, *refs):
    out_refs, field_ref = refs[:-1], refs[-1]
    freqs = sizes.freqs
    some = field_ref.shape[0] // 2
    member = lax.axis_index("beam").astype(jnp.int32) % sizes.group
    names = range(first, first + some)
    fields = []
    for b in names:
        mask = jnp.concatenate((mask_ref[b], mask_ref[b]), 1)
        masked = (spectrum_ref[0] * mask, spectrum_ref[1] * mask)
        field = combine(dot3((left_ref[b, 0], left_ref[b, 1]), masked), TILE, freqs)
        fields.append(split(jnp.concatenate(field, 0)))
    ends = []
    for b, field in zip(names, fields):
        field = combine(dot3(field, (right_ref[b, 0], right_ref[b, 1])), TILE, TILE)
        field = mul(field, mul((slice_ref[0], slice_ref[1]), (incident_ref[b, 0], incident_ref[b, 1])))
        ends.append(split(jnp.concatenate(field, 0)))
    turned = []
    for field in ends:
        field = combine(dot3(field, (last_x_ref[0, 0], last_x_ref[0, 1])), TILE, TILE)
        turned.append(split(jnp.concatenate(field, 1)))
    for n, field in enumerate(turned):
        field = combine(dot3((last_y_ref[0, 0], last_y_ref[0, 1]), field), TILE, TILE)
        for c in range(2):
            field_ref[2 * n + c] = field[c]
    rows = sizes.out_rows
    sets = sizes.group // sizes.share
    for other, out_ref in enumerate(out_refs):
        for k in range(sets):
            start = pl.multiple_of((member ^ other ^ (sizes.share * k)) * rows, rows)
            for n in range(2 * some):
                out_ref[k, n * rows:(n + 1) * rows] = field_ref[n, pl.ds(start, rows), :]


def probes_kernel(sizes, probes, weights_ref, *refs):
    field_refs, (out_ref, sums_ref, fields_ref) = refs[:-3], refs[-3:]
    sets, count = field_refs[0].shape[:2]
    for n, ref in enumerate(field_refs):
        for k in range(sets):
            fields_ref[k, n * count:(n + 1) * count] = ref[k]
    inner = fields_ref.shape[1] // sizes.out_rows
    weights = split(weights_ref[...])
    total = jnp.zeros((probes, TILE), jnp.float32)
    for k in range(sets):
        for row in range(sizes.out_rows):
            fields = split(fields_ref[k, pl.ds(row, inner, stride=sizes.out_rows), :])
            both = dot3(weights, fields)
            intensity = both[:probes] * both[:probes] + both[probes:] * both[probes:]
            if k == 0:
                out_ref[row] = intensity
            total = total + intensity
    sums_ref[...] = jnp.broadcast_to(jnp.sum(total, 1, keepdims=True), (probes, TILE))


def scale_kernel(intensity_ref, *refs):
    sums_refs, out_ref = refs[:-1], refs[-1]
    level = sums_refs[0][...]
    for ref in sums_refs[1:]:
        level = level + ref[...]
    level = level * (1.0 / (TILE * TILE)) + 1e-06
    out_ref[...] = intensity_ref[...] / level[None]


def per_device(potential, beam_tilts, aperture, aberration, probe_spots, crop_anchor, *, devices):
    sizes = Sizes(devices, potential.shape, beam_tilts.shape[0])
    rows, length, group, tiles, own = sizes.rows, sizes.length, sizes.group, sizes.tiles, sizes.own
    half, kept, freqs = sizes.half, sizes.kept, sizes.freqs
    member = lax.axis_index("beam").astype(jnp.int32) % group
    probes = probe_spots.shape[1]
    halves = 2 if own % 2 == 0 else 1
    some = own // halves

    def swap(value, bits):
        return lax.ppermute(value, "beam", [(i, i ^ bits) for i in range(devices)])

    def call(kernel, outs, specs, **kwargs):
        return pl.pallas_call(
            kernel,
            out_shape=outs,
            in_specs=specs,
            out_specs=kwargs.pop("out_specs", jax.tree.map(lambda _: VMEM, outs)),
            compiler_params=pltpu.CompilerParams(vmem_limit_bytes=16 << 20),
            **kwargs,
        )

    def half_type(*shape):
        return jax.ShapeDtypeStruct(shape, jnp.bfloat16)

    def full_type(*shape):
        return jax.ShapeDtypeStruct(shape, jnp.float32)

    def estimate(flops, bytes_accessed):
        return pl.CostEstimate(flops=flops, bytes_accessed=bytes_accessed, transcendentals=0)

    same, other_side = call(
        functools.partial(pack_kernel, sizes),
        (full_type(rows + sizes.piece_rows, length),) * 2,
        [VMEM, VMEM],
        cost_estimate=estimate(1 << 16, 1 << 18),
    )(crop_anchor[None], potential)
    blocks = [same]
    for shift in range(1, tiles):
        sent = same if shift % sizes.per_side == 0 else other_side
        blocks.append(swap(sent, shift * group))
    col_table, last_x = (jnp.asarray(table) for table in column_tables(sizes))
    small = pack_small(sizes, beam_tilts, aperture, aberration, probe_spots)
    fetched = [pltpu.SMEM(crop_anchor.shape, jnp.int32), pltpu.SMEM(small.shape, jnp.float32)]
    choice, row_table, left, last_y, incident, weights = call(
        functools.partial(early_tables_kernel, sizes, probes, halves),
        (
            jax.ShapeDtypeStruct((sizes.piece_rows, length), jnp.int32),
            half_type(2, 2, 2 * kept, half),
            half_type(own, 2, 2 * TILE, freqs),
            half_type(1, 2, 2 * TILE, TILE),
            full_type(own, 2, TILE, TILE),
            full_type(2 * probes, 2 * sizes.beams),
        ),
        [HBM] * 2,
        scratch_shapes=fetched + [pltpu.VMEM(small.shape, jnp.float32), pltpu.SemaphoreType.DMA((3,))],
        cost_estimate=estimate(1 << 22, 6 << 20),
    )(crop_anchor, small)
    right, masks = call(
        functools.partial(late_tables_kernel, sizes),
        (half_type(own, 2, freqs, 2 * TILE), half_type(own, freqs, freqs)),
        [HBM] * 2,
        scratch_shapes=fetched + [pltpu.SemaphoreType.DMA((2,))],
        cost_estimate=estimate(1 << 22, 6 << 20),
    )(crop_anchor, small)
    held = call(
        functools.partial(hold_kernel, sizes),
        full_type(sizes.block, length),
        [VMEM] * (1 + tiles),
        cost_estimate=estimate(1 << 16, 1 << 19),
    )(choice, *blocks)
    gathered = {0: held}
    for bits in member_steps(group):
        for ordinal in list(gathered):
            gathered[ordinal ^ bits] = swap(gathered[ordinal], bits)
    chunks = [
        [gathered[o] for o in range(low, low + sizes.chunk)] for low in range(0, group, sizes.chunk)
    ]

    spreads, pieces = [], []
    pairs = sizes.chunk * rows * tiles // 2
    for chunk in chunks[:-1]:
        spread, piece = call(
            functools.partial(spread_kernel, sizes),
            (half_type(2, 2, pairs, 2 * freqs), full_type(sizes.chunk * sizes.piece_rows, length)),
            [VMEM] * (sizes.chunk + 1),
            cost_estimate=estimate(pairs * half * half * 48, 2 << 20),
        )(*chunk, col_table)
        spreads.append(spread)
        pieces.append(piece)
    spectrum, slice_one = call(
        functools.partial(spectrum_kernel, sizes, len(spreads)),
        (half_type(2, freqs, 2 * freqs), full_type(2, TILE, TILE)),
        [VMEM] * (2 * len(spreads) + sizes.chunk + 2),
        cost_estimate=estimate(3 << 30, 4 << 20),
        scratch_shapes=[pltpu.VMEM((group * sizes.piece_rows, length), jnp.float32)],
    )(*spreads, *pieces, *chunks[-1], col_table, row_table)

    arrived = []
    sets = group // sizes.share
    for h in range(halves):
        fields = call(
            functools.partial(beams_kernel, sizes, h * some),
            (full_type(sets, 2 * some * sizes.out_rows, TILE),) * sizes.share,
            [VMEM] * 8,
            scratch_shapes=[pltpu.VMEM((2 * some, TILE, TILE), jnp.float32)],
            cost_estimate=estimate(some << 30, 4 << 20),
        )(spectrum, left, right, masks, last_x, last_y, slice_one, incident)
        arrived.append(fields[0])
        for other in range(1, sizes.share):
            arrived.append(swap(fields[other], other))

    intensity, total = call(
        functools.partial(probes_kernel, sizes, probes),
        (full_type(sizes.out_rows, probes, TILE), full_type(probes, TILE)),
        [VMEM] * (1 + len(arrived)),
        scratch_shapes=[pltpu.VMEM((sets, 2 * sizes.beams * sizes.out_rows, TILE), jnp.float32)],
        cost_estimate=estimate(1 << 26, 2 << 20),
    )(weights, *arrived)
    totals = [total]
    if sizes.share <= 4:
        for other in range(1, sizes.share):
            totals.append(swap(total, other))
    else:
        for bits in member_steps(sizes.share):
            total = total + swap(total, bits)
        totals = [total]
    return call(
        scale_kernel,
        full_type(sizes.out_rows, probes, TILE),
        [VMEM] * (1 + len(totals)),
        cost_estimate=estimate(1 << 18, 1 << 20),
    )(intensity, *totals)


def pack_small(sizes, beam_tilts, aperture, aberration, probe_spots):
    probes = probe_spots.shape[1]
    width = max(sizes.beams, probes)
    spots = probe_spots.transpose(0, 2, 1).reshape(2 * sizes.tiles, probes).astype(jnp.float32)
    beams = jnp.concatenate((beam_tilts.T.astype(jnp.float32), aperture[None], aberration[None]), 0)
    return jnp.concatenate(
        (
            jnp.pad(beams, ((0, 0), (0, width - sizes.beams))),
            jnp.pad(spots, ((0, 0), (0, width - probes))),
        ),
        0,
    )


def member_steps(group):
    return [group >> (i + 1) for i in range(group.bit_length() - 1)]


def solution(mesh):
    placed = (P("groups", "beam", None), P(), P(), P(), P("groups", None, None), P("groups"))

    devices = mesh.shape["beam"]

    def body(*args):
        return per_device(*args, devices=devices)

    return jax.shard_map(
        body,
        mesh=mesh,
        in_specs=placed,
        out_specs=P(("groups", "beam"), None, None),
        check_vma=False,
    )
```
